512 devices in a mesh: obs: 8 (over y), grid: 64 (over z, x, core).
Axes of the slice: x: 4, y: 8, z: 8, core: 2. Of those that a mesh axis runs over, the one named last changes fastest.
Arguments:
- adjoint_start: float32 [256, 8, 1024, 128], P('obs', None, 'grid'), may hold values from -2 to 2
- conductance: float32 [2, 8, 1024, 128], P(None, 'obs', 'grid'), may hold values from 0.2 to 5
- storage: float32 [8, 1024, 128], P('obs', 'grid'), may hold values from 0.5 to 2
- head: float32 [8, 1024, 128], P('obs', 'grid'), may hold values from -6 to 6
- layer_open: int32 [8, 1024, 128], P(None, 'grid'), may hold values 0 or 1
- krig_weight: float32 [4, 8, 1024, 128], P(None, 'obs', 'grid'), may hold values from 0.05 to 0.45
- krig_pilot: int32 [4, 8, 1024, 128], P(None, None, 'grid'), may hold values from 0 to 8191, as said below
- obs_cell: int32 [256, 2], P('obs'), may hold values from 0 to 1048575
- obs_weight: float32 [256, 2], P('obs'), may hold values from -8 to 8
Outputs:
- jacobian: float32 [2, 256, 8192], P(None, 'obs', 'grid')
The draws below stay inside these ranges and needn't reach their ends.
Inputs may be any that keep to these rules, and one draw needn't show every extreme that they name: `krig_pilot`: owner block b holds the pilot points b * 128 to (b + 1) * 128 - 1. Every stencil member of a cell in column x lies in an owner block from t - 2 to t + 2, with t = x // 16.
All inputs are finite; a program needn't handle non-finite values. No bound on the sum of `layer_open` on one device may be relied on, other than what follows from the above.
Results may differ from the reference program's by a relative error of at most 0.00026.
Values sent between devices are 32-bit elements; how exact they have to be, the bound alone decides.
No kernel may reach another device: no remote copies, remote signals or barrier semaphores. Data moves between devices by JAX's collectives and lax.ppermute only.
A program may use at most 64 MiB of HBM per device.

```python
import math
import jax
import jax.numpy as jnp
from jax import lax

LAY = 8
NK = 4
RADIUS = 2
OBS_DEV = 32
TX = 16
TY = 128
P_DEV = 128
OBS = 256
NX = 1024
PILOTS = 8192
N_OBS = 8


def draw_krig_pilot(key, part):
    tiles = NX // TX
    key_span, key_offset, key_member = jax.random.split(key, 3)
    span_tile = jax.random.randint(key_span, (tiles,), 0, RADIUS + 1)
    tile_index = jnp.arange(NX, dtype=jnp.int32) // TX
    span_cell = span_tile[tile_index][None, None, :, None]
    offsets = jax.random.randint(key_offset, (NK, LAY, NX, TY), -span_cell, span_cell + 1)
    owners = jnp.clip(tile_index[None, None, :, None] + offsets, 0, tiles - 1)
    pilot_ids = owners * P_DEV + jax.random.randint(key_member, (NK, LAY, NX, TY), 0, P_DEV)
    pilot_ids = pilot_ids.at[0, 0, 0, 0].set(0)
    pilot_ids = pilot_ids.at[NK - 1, LAY - 1, NX - 1, TY - 1].set(tiles * P_DEV - 1)
    return pilot_ids.astype(jnp.int32)


def set_ends(entries, rng, low, top_value):
    place = [jax.random.randint(jax.random.fold_in(rng, axis), (), 0, length) for axis, length in enumerate(entries.shape)]
    widest = entries.shape.index(max(entries.shape))
    next_to = place[:widest] + [(place[widest] + 1) % entries.shape[widest]] + place[widest + 1:]
    return entries.at[tuple(place)].set(low).at[tuple(next_to)].set(top_value)


def level_of(own_key, extent, cuts, low, top_value):
    gain, own = 1.0, jax.random.fold_in(own_key, 6)
    for position, parts in cuts:
        draws = jnp.exp(jax.random.uniform(jax.random.fold_in(own, position), (parts,), jnp.float32, low / len(cuts), top_value / len(cuts)))
        gain = gain * jnp.repeat(draws, extent[position] // parts).reshape([-1 if axis == position else 1 for axis in range(len(extent))])
    return gain


def noise(key, shape, spread, reach, cuts=(), kind=jnp.bfloat16):
    values = jax.random.normal(key, shape, jnp.float32) * spread
    if len(cuts) > 0:
        values = level_of(key, shape, cuts, -0.22, 0.18) * values
    return jnp.clip(values, min=-reach, max=reach).astype(kind)


def setup_inputs(seed: int = 0) -> dict:
    key_list = jax.random.split(jax.random.key(seed), 10)
    adjoint_start = noise(key_list[0], (OBS, LAY, NX, TY), 0.25, 2.0, ((0, 8), (2, 64)), jnp.float32)
    conductance = jnp.clip(jnp.exp(math.log(5.0) - 3.218876 * jax.random.uniform(key_list[1], (2, LAY, NX, TY), jnp.float32) ** level_of(key_list[1], (2, LAY, NX, TY), ((1, 8), (2, 64)), -0.2, 0.2)), 0.2, 5.0)
    storage = jnp.clip(jnp.exp(math.log(2.0) - 1.3862944 * jax.random.uniform(key_list[2], (LAY, NX, TY), jnp.float32) ** level_of(key_list[2], (LAY, NX, TY), ((0, 8), (1, 64)), -0.2, 0.2)), 0.5, 2.0)
    head = noise(key_list[3], (LAY, NX, TY), 1.0, 6.0, ((0, 8), (1, 64)), jnp.float32)
    layer_open = set_ends((jax.random.randint(key_list[4], (LAY, NX, TY), 0, 4) < 3).astype(jnp.int32), jax.random.fold_in(key_list[4], 1), 0, 1)
    krig_weight = jnp.clip(0.05 + 0.39999999 * jax.random.uniform(key_list[5], (NK, LAY, NX, TY), jnp.float32) ** level_of(key_list[5], (NK, LAY, NX, TY), ((1, 8), (2, 64)), -0.2, 0.2), 0.05, 0.45)
    krig_pilot = draw_krig_pilot(jax.random.fold_in(key_list[9], 71), 0)
    obs_cell = set_ends(jax.random.randint(key_list[7], (OBS, 2), 0, LAY * NX * TY), jax.random.fold_in(key_list[7], 1), 0, (LAY * NX * TY) - 1).astype(jnp.int32)
    obs_weight = noise(key_list[8], (OBS, 2), 2.0, 8.0, ((0, 8),), jnp.float32)
    return {"adjoint_start": adjoint_start, "conductance": conductance, "storage": storage, "head": head, "layer_open": layer_open, "krig_weight": krig_weight, "krig_pilot": krig_pilot, "obs_cell": obs_cell, "obs_weight": obs_weight}


OMEGA = 0.8


def harmonic(k_first, k_second):
    total = k_first + k_second
    return (2.0 * k_first * k_second / total,
            2.0 * k_first * k_second * k_second / (total * total),
            2.0 * k_second * k_first * k_first / (total * total))


def lower_upper(face, axis):
    low_pad = [(0, 0)] * face.ndim
    high_pad = [(0, 0)] * face.ndim
    low_pad[axis] = (0, 1)
    high_pad[axis] = (1, 0)
    return jnp.pad(face, low_pad), jnp.pad(face, high_pad)


def apply_darcy(adjoint, medium, live):
    live_b = live[None, :, None]
    k_horiz = jnp.where(live_b > 0, medium[0], 1.0)
    k_vert = jnp.where(live_b > 0, medium[1], 1.0)
    storage_c = jnp.where(live_b > 0, medium[2], 1.0)
    face_x = harmonic(k_horiz[:, :-1], k_horiz[:, 1:])[0] * live_b[:, :-1] * live_b[:, 1:]
    face_y = harmonic(k_horiz[:, :, :-1], k_horiz[:, :, 1:])[0]
    face_z = harmonic(k_vert[:-1], k_vert[1:])[0] * medium[4][:-1]
    pair_x = lower_upper(face_x, 1)
    pair_y = lower_upper(face_y, 2)
    pair_z = lower_upper(face_z, 0)
    diagonal = storage_c + pair_x[0] + pair_x[1] + pair_y[0] + pair_y[1] + pair_z[0] + pair_z[1]
    flux_x = lower_upper(face_x * (adjoint[:, :, :-1] - adjoint[:, :, 1:]), 2)
    flux_y = lower_upper(face_y * (adjoint[:, :, :, :-1] - adjoint[:, :, :, 1:]), 3)
    flux_z = lower_upper(face_z * (adjoint[:, :-1] - adjoint[:, 1:]), 1)
    applied = storage_c * adjoint + flux_x[0] - flux_x[1] + flux_y[0] - flux_y[1] + flux_z[0] - flux_z[1]
    return applied, diagonal


def jacobi(adjoint, medium, live, source):
    applied, diagonal = apply_darcy(adjoint, medium, live)
    return (adjoint + OMEGA * (source - applied) / diagonal) * live[None, None, :, None]


def sensitivity(adjoint, medium, live):
    live_b = live[None, :, None]
    k_horiz = jnp.where(live_b > 0, medium[0], 1.0)
    k_vert = jnp.where(live_b > 0, medium[1], 1.0)
    head_c = medium[3]
    unused_x, lower_x, upper_x = harmonic(k_horiz[:, :-1], k_horiz[:, 1:])
    mask_x = live_b[:, :-1] * live_b[:, 1:]
    prod_x = (adjoint[:, :, :-1] - adjoint[:, :, 1:]) * (head_c[:, :-1] - head_c[:, 1:]) * mask_x
    unused_y, lower_y, upper_y = harmonic(k_horiz[:, :, :-1], k_horiz[:, :, 1:])
    prod_y = (adjoint[:, :, :, :-1] - adjoint[:, :, :, 1:]) * (head_c[:, :, :-1] - head_c[:, :, 1:])
    unused_z, lower_z, upper_z = harmonic(k_vert[:-1], k_vert[1:])
    prod_z = (adjoint[:, :-1] - adjoint[:, 1:]) * (head_c[:-1] - head_c[1:]) * medium[4][:-1]
    horiz = (lower_upper(lower_x * prod_x, 2)[0] + lower_upper(upper_x * prod_x, 2)[1]
             + lower_upper(lower_y * prod_y, 3)[0] + lower_upper(upper_y * prod_y, 3)[1])
    vert = lower_upper(lower_z * prod_z, 1)[0] + lower_upper(upper_z * prod_z, 1)[1]
    return jnp.stack([-horiz, -vert])


def reference(adjoint_start, conductance, storage, head, layer_open, krig_weight, krig_pilot, obs_cell, obs_weight):
    medium = jnp.stack([conductance[0], conductance[1], storage, head, layer_open.astype(jnp.float32)])
    live = jnp.ones((NX,), jnp.float32)
    flat_ids = krig_pilot.reshape(NK, -1)
    flat_weights = krig_weight.reshape(NK, -1)

    def one_group(group):
        start, cells, weights = group
        count = start.shape[0]
        rows_idx = jnp.arange(count, dtype=jnp.int32)[:, None]
        source = jnp.zeros((count, LAY * NX * TY), jnp.float32).at[rows_idx, cells].add(weights)
        source = source.reshape(count, LAY, NX, TY)
        adjoint = jacobi(start, medium, live, source)
        adjoint = jacobi(adjoint, medium, live, source)
        sens = sensitivity(adjoint, medium, live)
        sens_flat = sens.reshape(2 * count, -1).T
        total = jnp.zeros((PILOTS, 2 * count), jnp.float32)
        for member in range(NK):
            total = total + jax.ops.segment_sum(sens_flat * flat_weights[member][:, None], flat_ids[member], num_segments=PILOTS)
        return total.T.reshape(2, count, PILOTS)

    groups = (adjoint_start.reshape(N_OBS, OBS_DEV, LAY, NX, TY),
              obs_cell.reshape(N_OBS, OBS_DEV, 2),
              obs_weight.reshape(N_OBS, OBS_DEV, 2))
    result = lax.map(one_group, groups)
    return jnp.transpose(result, (1, 0, 2, 3)).reshape(2, OBS, PILOTS)
```

```python
import jax
import jax.numpy as jnp
from jax import lax
from jax.experimental import pallas as pl
from jax.experimental.pallas import tpu as pltpu
from jax.sharding import PartitionSpec as P

NK = 4
RADIUS = 2
P_DEV = 128
OMEGA = 0.8
LAY = 8
OBS = 32
TX = 16
TY = 128
HALO = 3
SPAN = (2 * RADIUS + 1) * P_DEV
OFF = 8
EXT = 32
KX = 4

F32 = jnp.float32
BF16 = jnp.bfloat16
I16 = jnp.int16
VMEM = pl.BlockSpec(memory_space=pltpu.VMEM)
SMEM = pl.BlockSpec(memory_space=pltpu.SMEM)


def edges_kernel(adj_ref, low_ref, high_ref):
    stride = LAY * TX

    def body(layer, carry):
        for j in range(HALO):
            low_ref[layer, j] = adj_ref[pl.ds(layer * TX + j, OBS, stride=stride), :]
            high_ref[layer, j] = adj_ref[
                pl.ds(layer * TX + TX - HALO + j, OBS, stride=stride), :
            ]
        return carry

    lax.fori_loop(0, LAY, body, 0)


def medium_edges_kernel(med_ref, open_ref, low_ref, high_ref):
    for layer in range(LAY):
        for field in range(5):
            if field < 4:
                tile = med_ref[layer, field]
            else:
                tile = open_ref[layer].astype(F32)
            low_ref[layer, pl.ds(field * HALO, HALO), :] = tile[:HALO]
            high_ref[layer, pl.ds(field * HALO, HALO), :] = tile[TX - HALO :]
        low_ref[layer, pl.ds(15, 1), :] = jnp.zeros((1, TY), F32)
        high_ref[layer, pl.ds(15, 1), :] = jnp.zeros((1, TY), F32)


def stencil_kernel(
    tile_ref,
    adj_ref,
    low_ref,
    high_ref,
    med_ref,
    open_ref,
    med_low_ref,
    med_high_ref,
    cell_ref,
    weight_ref,
    out_ref,
    ext_ref,
    coef_ref,
    grad_ref,
    start_ref,
    one_ref,
    two_ref,
):
    tile = tile_ref[0, 0]
    n_tiles = tile_ref[0, 1]
    whole_x = n_tiles * TX

    row = lax.broadcasted_iota(jnp.int32, (EXT, TY), 0)
    lane = lax.broadcasted_iota(jnp.int32, (EXT, TY), 1)
    global_x = tile * TX + row - OFF
    live = (global_x >= 0) & (global_x < whole_x)
    live_next = (global_x + 1 >= 0) & (global_x + 1 < whole_x)
    both = jnp.where(live & live_next, 1.0, 0.0).astype(F32)
    for layer in range(LAY):
        for field in range(5):
            fill = jnp.ones((OFF, TY), F32)
            ext_ref[field, layer, pl.ds(0, OFF), :] = fill
            ext_ref[field, layer, pl.ds(OFF + TX, OFF), :] = fill
            own = med_ref[layer, field] if field < 4 else open_ref[layer].astype(F32)
            ext_ref[field, layer, pl.ds(OFF, TX), :] = own
            ext_ref[field, layer, pl.ds(OFF - HALO, HALO), :] = med_low_ref[
                layer, pl.ds(field * HALO, HALO), :
            ]
            ext_ref[field, layer, pl.ds(OFF + TX, HALO), :] = med_high_ref[
                layer, pl.ds(field * HALO, HALO), :
            ]

    stride = LAY * TX

    def gather(layer, carry):
        for j in range(HALO):
            start_ref[layer, j] = low_ref[layer, j]
            start_ref[layer, HALO + TX + j] = high_ref[layer, j]
        for x in range(TX):
            start_ref[layer, HALO + x] = adj_ref[pl.ds(layer * TX + x, OBS, stride=stride), :]
        return carry

    lax.fori_loop(0, LAY, gather, 0)

    def medium(field, layer):
        value = ext_ref[field, layer]
        if field < 3:
            return jnp.where(live, value, 1.0)
        return value

    def below(value):
        return pltpu.roll(value, 1, 0)

    def above(value):
        return pltpu.roll(value, EXT - 1, 0)

    def west(value):
        return pltpu.roll(value, 1, 1)

    def east(value):
        return pltpu.roll(value, TY - 1, 1)

    has_west = jnp.where(lane > 0, 1.0, 0.0).astype(F32)
    has_east = jnp.where(lane < TY - 1, 1.0, 0.0).astype(F32)
    before = below(both)

    def pair(mine, other):
        inv = 1.0 / (mine + other)
        face = 2.0 * mine * other * inv
        return face, face * other * inv

    for layer in range(LAY):
        k = medium(0, layer)
        kv = medium(1, layer)
        head = medium(3, layer)
        fxm, gxm = pair(k, below(k))
        fxp, gxp = pair(k, above(k))
        fym, gym = pair(k, west(k))
        fyp, gyp = pair(k, east(k))
        fxm = fxm * before
        fxp = fxp * both
        fym = fym * has_west
        fyp = fyp * has_east
        diag = medium(2, layer) + fxm + fxp + fym + fyp
        zero = jnp.zeros((EXT, TY), F32)
        fzm = fzp = gzm = gzp = zero
        if layer > 0:
            fzm, gzm = pair(kv, medium(1, layer - 1))
            gate = ext_ref[4, layer - 1]
            fzm = fzm * gate
            gzm = gzm * gate * (head - medium(3, layer - 1))
        if layer < LAY - 1:
            fzp, gzp = pair(kv, medium(1, layer + 1))
            gate = ext_ref[4, layer]
            fzp = fzp * gate
            gzp = gzp * gate * (head - medium(3, layer + 1))
        diag = diag + fzm + fzp
        scale = OMEGA / diag
        for n, value in enumerate((fxm, fxp, fym, fyp, fzm, fzp)):
            coef_ref[n, layer] = value * scale
        coef_ref[6, layer] = scale
        grad_ref[0, layer] = gxm * before * (head - below(head))
        grad_ref[1, layer] = gxp * both * (head - above(head))
        grad_ref[2, layer] = gym * has_west * (head - west(head))
        grad_ref[3, layer] = gyp * has_east * (head - east(head))
        grad_ref[4, layer] = gzm
        grad_ref[5, layer] = gzp

    lanes = lax.broadcasted_iota(jnp.int32, (OBS, TY), 1)
    target = [
        jnp.broadcast_to(cell_ref[:, pl.ds(m, 1)], (OBS, TY)) - lanes for m in range(2)
    ]
    amount = [jnp.broadcast_to(weight_ref[:, pl.ds(m, 1)], (OBS, TY)) for m in range(2)]

    def rows(ref, n, layer, x):
        return jnp.broadcast_to(ref[n, layer, pl.ds(x + OFF, 1), :], (OBS, TY))

    def sweep(src_ref, dst_ref, margin):
        def body(layer, carry):
            down = jnp.maximum(layer - 1, 0)
            up = jnp.minimum(layer + 1, LAY - 1)
            for x in range(-margin, TX + margin):
                j = x + margin + 1
                mid = src_ref[layer, j]
                base = (layer * whole_x + tile * TX + x) * TY
                source = jnp.where(target[0] == base, amount[0], 0.0) + jnp.where(
                    target[1] == base, amount[1], 0.0
                )
                value = (1.0 - OMEGA) * mid + rows(coef_ref, 6, layer, x) * source
                value += rows(coef_ref, 0, layer, x) * src_ref[layer, j - 1]
                value += rows(coef_ref, 1, layer, x) * src_ref[layer, j + 1]
                value += rows(coef_ref, 2, layer, x) * pltpu.roll(mid, 1, 1)
                value += rows(coef_ref, 3, layer, x) * pltpu.roll(mid, TY - 1, 1)
                value += rows(coef_ref, 4, layer, x) * src_ref[down, j]
                value += rows(coef_ref, 5, layer, x) * src_ref[up, j]
                dst_ref[layer, j - 1] = value
            return carry

        lax.fori_loop(0, LAY, body, 0)

    sweep(start_ref, one_ref, 2)
    sweep(one_ref, two_ref, 1)

    def split(value):
        high = value.astype(BF16)
        return high, (value - high.astype(F32)).astype(BF16)

    def sense(layer, carry):
        down = jnp.maximum(layer - 1, 0)
        up = jnp.minimum(layer + 1, LAY - 1)
        for x in range(TX):
            j = x + 1
            mid = two_ref[layer, j]
            horiz = rows(grad_ref, 0, layer, x) * (two_ref[layer, j - 1] - mid)
            horiz += rows(grad_ref, 1, layer, x) * (two_ref[layer, j + 1] - mid)
            horiz += rows(grad_ref, 2, layer, x) * (pltpu.roll(mid, 1, 1) - mid)
            horiz += rows(grad_ref, 3, layer, x) * (pltpu.roll(mid, TY - 1, 1) - mid)
            vert = rows(grad_ref, 4, layer, x) * (two_ref[down, j] - mid)
            vert += rows(grad_ref, 5, layer, x) * (two_ref[up, j] - mid)
            chunk = layer * (TX // 2) + x // 2
            half = pl.ds((x % 2) * TY, TY)
            for field, value in enumerate((horiz, vert)):
                high, low = split(value)
                out_ref[chunk, pl.ds(field * OBS, OBS), half] = high
                out_ref[chunk, pl.ds((2 + field) * OBS, OBS), half] = low
        return carry

    lax.fori_loop(0, LAY, sense, 0)


def krig_kernel(tile_ref, sens_ref, pilot_ref, weight_ref, *rest):
    outs = rest[:5]
    index_ref, share_ref, first_ref, second_ref, total_ref = rest[5:]
    base = (tile_ref[0, 0] - RADIUS) * P_DEV
    chunks = LAY * TX // KX

    for layer in range(LAY):
        index = [pilot_ref[k, layer] - base for k in range(NK)]
        share = [weight_ref[layer, k] for k in range(NK)]
        for k in range(1, NK):
            for j in range(k):
                same = index[j] == index[k]
                share[j] = share[j] + jnp.where(same, share[k], 0.0)
                index[k] = jnp.where(same, -1, index[k])
        for k in range(NK):
            index_ref[pl.ds(layer * TX, TX), k, :] = index[k]
            share_ref[pl.ds(layer * TX, TX), k, :] = share[k]

    iota = lax.broadcasted_iota(I16, (16, TY), 0)

    def build(chunk, matrix_ref):
        for s in range(KX):
            row = chunk * KX + s
            index = []
            high = []
            low = []
            for k in range(NK):
                index.append(
                    jnp.broadcast_to(index_ref[row, pl.ds(k, 1), :], (16, TY)).astype(I16)
                )
                share = jnp.broadcast_to(share_ref[row, pl.ds(k, 1), :], (16, TY))
                top = share.astype(BF16)
                high.append(top)
                low.append((share - top.astype(F32)).astype(BF16))
            for i in range(SPAN // 16):
                pilot = iota + I16(16 * i)
                upper = jnp.zeros((16, TY), BF16)
                lower = jnp.zeros((16, TY), BF16)
                for k in range(NK):
                    hit = index[k] == pilot
                    upper = jnp.where(hit, high[k], upper)
                    lower = jnp.where(hit, low[k], lower)
                matrix_ref[pl.ds(16 * i, 16), pl.ds(TY * s, TY)] = upper
                matrix_ref[pl.ds(SPAN + 16 * i, 16), pl.ds(TY * s, TY)] = lower

    def add(chunk, matrix_ref):
        sens = jnp.concatenate([sens_ref[chunk * (KX // 2) + q] for q in range(KX // 2)], axis=1)
        total_ref[...] += lax.dot_general(
            matrix_ref[...], sens, (((1,), (1,)), ((), ())), preferred_element_type=F32
        )

    total_ref[...] = jnp.zeros_like(total_ref)
    build(0, first_ref)

    def body(i, carry):
        add(2 * i, first_ref)
        build(2 * i + 1, second_ref)
        add(2 * i + 1, second_ref)
        build(jnp.minimum(2 * i + 2, chunks - 1), first_ref)
        return carry

    lax.fori_loop(0, chunks // 2, body, 0)
    for o in range(5):
        piece = total_ref[pl.ds(o * P_DEV, P_DEV), :] + total_ref[pl.ds(SPAN + o * P_DEV, P_DEV), :]
        piece = piece.T
        outs[o][...] = piece[: 2 * OBS] + piece[2 * OBS :]


def shift(block, axis, by):
    count = lax.axis_size(axis)
    pairs = [(i, i + by) for i in range(count) if 0 <= i + by < count]
    return lax.ppermute(block, axis, pairs)


def gathered(block, axis):
    count = lax.axis_size(axis)
    return lax.all_to_all(
        jnp.broadcast_to(block[None], (count,) + block.shape), axis, 0, 0, tiled=False
    )


def shards(
    adjoint_start,
    conductance,
    storage,
    head,
    layer_open,
    krig_weight,
    krig_pilot,
    obs_cell,
    obs_weight,
):
    sds = jax.ShapeDtypeStruct
    limit = pltpu.CompilerParams(vmem_limit_bytes=52 * 2**20)
    tile = jnp.stack(
        [lax.axis_index("grid"), jnp.int32(lax.axis_size("grid"))]
    ).reshape(1, 2)

    own = jnp.concatenate([conductance[:, 0], storage, head], axis=0)
    medium = gathered(own, "obs")

    flat_adjoint = adjoint_start.reshape(OBS * LAY * TX, TY)
    edge = sds((LAY, HALO, OBS, TY), F32)
    low, high = pl.pallas_call(
        edges_kernel, out_shape=(edge, edge), in_specs=[VMEM], out_specs=(VMEM, VMEM)
    )(flat_adjoint)
    from_low = shift(high, "grid", 1)
    from_high = shift(low, "grid", -1)

    share = gathered(krig_weight[:, 0], "obs")

    edge = sds((LAY, 16, TY), F32)
    med_low, med_high = pl.pallas_call(
        medium_edges_kernel,
        out_shape=(edge, edge),
        in_specs=[VMEM, VMEM],
        out_specs=(VMEM, VMEM),
    )(medium, layer_open)
    med_from_low = shift(med_high, "grid", 1)
    med_from_high = shift(med_low, "grid", -1)

    sens = pl.pallas_call(
        stencil_kernel,
        out_shape=sds((LAY * TX // 2, 4 * OBS, 2 * TY), BF16),
        in_specs=[SMEM] + [VMEM] * 9,
        out_specs=VMEM,
        scratch_shapes=[
            pltpu.VMEM((5, LAY, EXT, TY), F32),
            pltpu.VMEM((7, LAY, EXT, TY), F32),
            pltpu.VMEM((6, LAY, EXT, TY), F32),
            pltpu.VMEM((LAY, TX + 6, OBS, TY), F32),
            pltpu.VMEM((LAY, TX + 4, OBS, TY), F32),
            pltpu.VMEM((LAY, TX + 2, OBS, TY), F32),
        ],
        compiler_params=limit,
    )(
        tile,
        flat_adjoint,
        from_low,
        from_high,
        medium,
        layer_open,
        med_from_low,
        med_from_high,
        obs_cell,
        obs_weight,
    )

    piece = sds((2 * OBS, P_DEV), F32)
    pieces = pl.pallas_call(
        krig_kernel,
        out_shape=[piece] * 5,
        in_specs=[SMEM] + [VMEM] * 3,
        out_specs=[VMEM] * 5,
        scratch_shapes=[
            pltpu.VMEM((LAY * TX, NK, TY), jnp.int32),
            pltpu.VMEM((LAY * TX, NK, TY), F32),
            pltpu.VMEM((2 * SPAN, KX * TY), BF16),
            pltpu.VMEM((2 * SPAN, KX * TY), BF16),
            pltpu.VMEM((2 * SPAN, 4 * OBS), F32),
        ],
        compiler_params=limit,
    )(tile, sens, krig_pilot, share)

    owned = pieces[RADIUS]
    for offset in (0, 4, 1, 3):
        owned = owned + shift(pieces[offset], "grid", offset - RADIUS)
    return owned.reshape(2, OBS, P_DEV)


def solution(mesh):
    return jax.shard_map(
        shards,
        mesh=mesh,
        in_specs=(
            P("obs", None, "grid", None),
            P(None, "obs", "grid", None),
            P("obs", "grid", None),
            P("obs", "grid", None),
            P(None, "grid", None),
            P(None, "obs", "grid", None),
            P(None, None, "grid", None),
            P("obs", None),
            P("obs", None),
        ),
        out_specs=P(None, "obs", "grid"),
        check_vma=False,
    )
```

```python
import jax
import jax.numpy as jnp
from jax import lax
from jax.experimental import pallas as pl
from jax.experimental.pallas import tpu as pltpu
from jax.sharding import PartitionSpec as P

NK = 4
RADIUS = 2
P_DEV = 128
OMEGA = 0.8
LAY = 8
OBS = 32
TX = 16
TY = 128
HALO = 3
SPAN = (2 * RADIUS + 1) * P_DEV
OFF = 8
EXT = 32
KX = 16

F32 = jnp.float32
BF16 = jnp.bfloat16
I16 = jnp.int16
VMEM = pl.BlockSpec(memory_space=pltpu.VMEM)
SMEM = pl.BlockSpec(memory_space=pltpu.SMEM)


def turn_kernel(tile_ref, adj_ref, turned_ref, pair_ref, other_ref):
    stride = LAY * TX
    odd = tile_ref[0, 0] % 2
    pair_start = (1 - odd) * (TX - HALO)
    other_start = odd * (TX - HALO)

    def body(layer, carry):
        for x in range(TX):
            turned_ref[layer, x] = adj_ref[pl.ds(layer * TX + x, OBS, stride=stride), :]
        for j in range(HALO):
            pair_ref[layer, j] = turned_ref[layer, pair_start + j]
            other_ref[layer, j] = turned_ref[layer, other_start + j]
        return carry

    lax.fori_loop(0, LAY, body, 0)


def medium_edges_kernel(tile_ref, med_ref, open_ref, pair_ref, other_ref):
    odd = tile_ref[0, 0] % 2 == 1
    for layer in range(LAY):
        for field in range(5):
            if field < 4:
                tile = med_ref[layer, field]
            else:
                tile = open_ref[layer].astype(F32)
            low = tile[:HALO]
            high = tile[TX - HALO :]
            rows = pl.ds(field * HALO, HALO)
            pair_ref[layer, rows, :] = jnp.where(odd, low, high)
            other_ref[layer, rows, :] = jnp.where(odd, high, low)
        pair_ref[layer, pl.ds(15, 1), :] = jnp.zeros((1, TY), F32)
        other_ref[layer, pl.ds(15, 1), :] = jnp.zeros((1, TY), F32)


def stencil_kernel(
    tile_ref,
    turned_ref,
    pair_ref,
    other_ref,
    med_ref,
    open_ref,
    med_pair_ref,
    med_other_ref,
    cell_ref,
    weight_ref,
    out_ref,
    ext_ref,
    coef_ref,
    grad_ref,
    halo_ref,
    one_ref,
    two_ref,
):
    tile = tile_ref[0, 0]
    n_tiles = tile_ref[0, 1]
    whole_x = n_tiles * TX
    odd = tile % 2

    row = lax.broadcasted_iota(jnp.int32, (EXT, TY), 0)
    lane = lax.broadcasted_iota(jnp.int32, (EXT, TY), 1)
    global_x = tile * TX + row - OFF
    live = (global_x >= 0) & (global_x < whole_x)
    live_next = (global_x + 1 >= 0) & (global_x + 1 < whole_x)
    both = jnp.where(live & live_next, 1.0, 0.0).astype(F32)
    for layer in range(LAY):
        for field in range(5):
            fill = jnp.ones((OFF, TY), F32)
            ext_ref[field, layer, pl.ds(0, OFF), :] = fill
            ext_ref[field, layer, pl.ds(OFF + TX, OFF), :] = fill
            own = med_ref[layer, field] if field < 4 else open_ref[layer].astype(F32)
            ext_ref[field, layer, pl.ds(OFF, TX), :] = own
            pair = med_pair_ref[layer, pl.ds(field * HALO, HALO), :]
            other = med_other_ref[layer, pl.ds(field * HALO, HALO), :]
            ext_ref[field, layer, pl.ds(OFF - HALO, HALO), :] = jnp.where(odd == 1, pair, other)
            ext_ref[field, layer, pl.ds(OFF + TX, HALO), :] = jnp.where(odd == 1, other, pair)

    def place(layer, carry):
        for j in range(HALO):
            halo_ref[layer, HALO * (1 - odd) + j] = pair_ref[layer, j]
            halo_ref[layer, HALO * odd + j] = other_ref[layer, j]
        return carry

    lax.fori_loop(0, LAY, place, 0)

    def medium(field, layer):
        value = ext_ref[field, layer]
        if field < 3:
            return jnp.where(live, value, 1.0)
        return value

    def below(value):
        return pltpu.roll(value, 1, 0)

    def above(value):
        return pltpu.roll(value, EXT - 1, 0)

    def west(value):
        return pltpu.roll(value, 1, 1)

    def east(value):
        return pltpu.roll(value, TY - 1, 1)

    has_west = jnp.where(lane > 0, 1.0, 0.0).astype(F32)
    has_east = jnp.where(lane < TY - 1, 1.0, 0.0).astype(F32)
    before = below(both)

    def faces(mine, other):
        inv = 1.0 / (mine + other)
        face = 2.0 * mine * other * inv
        return face, face * other * inv

    for layer in range(LAY):
        k = medium(0, layer)
        kv = medium(1, layer)
        head = medium(3, layer)
        fxm, gxm = faces(k, below(k))
        fxp, gxp = faces(k, above(k))
        fym, gym = faces(k, west(k))
        fyp, gyp = faces(k, east(k))
        fxm = fxm * before
        fxp = fxp * both
        fym = fym * has_west
        fyp = fyp * has_east
        diag = medium(2, layer) + fxm + fxp + fym + fyp
        zero = jnp.zeros((EXT, TY), F32)
        fzm = fzp = gzm = gzp = zero
        if layer > 0:
            fzm, gzm = faces(kv, medium(1, layer - 1))
            gate = ext_ref[4, layer - 1]
            fzm = fzm * gate
            gzm = gzm * gate * (head - medium(3, layer - 1))
        if layer < LAY - 1:
            fzp, gzp = faces(kv, medium(1, layer + 1))
            gate = ext_ref[4, layer]
            fzp = fzp * gate
            gzp = gzp * gate * (head - medium(3, layer + 1))
        diag = diag + fzm + fzp
        scale = OMEGA / diag
        for n, value in enumerate((fxm, fxp, fym, fyp, fzm, fzp)):
            coef_ref[n, layer] = value * scale
        coef_ref[6, layer] = scale
        grad_ref[0, layer] = gxm * before * (head - below(head))
        grad_ref[1, layer] = gxp * both * (head - above(head))
        grad_ref[2, layer] = gym * has_west * (head - west(head))
        grad_ref[3, layer] = gyp * has_east * (head - east(head))
        grad_ref[4, layer] = gzm
        grad_ref[5, layer] = gzp

    lanes = lax.broadcasted_iota(jnp.int32, (OBS, TY), 1)
    eye = lax.broadcasted_iota(jnp.int32, (OBS, OBS), 0) == lax.broadcasted_iota(
        jnp.int32, (OBS, OBS), 1
    )

    def column(row):
        square = jnp.where(eye, jnp.broadcast_to(row, (OBS, OBS)), 0.0)
        return jnp.broadcast_to(jnp.sum(square, axis=1, keepdims=True), (OBS, TY))

    target = [
        column(cell_ref[pl.ds(m, 1), :].astype(F32)).astype(jnp.int32) - lanes for m in range(2)
    ]
    amount = [column(weight_ref[pl.ds(m, 1), :]) for m in range(2)]

    def rows(ref, n, layer, x):
        return jnp.broadcast_to(ref[n, layer, pl.ds(x + OFF, 1), :], (OBS, TY))

    def start(layer, j):
        if j < HALO:
            return halo_ref[layer, j]
        if j < HALO + TX:
            return turned_ref[layer, j - HALO]
        return halo_ref[layer, j - TX]

    def sweep(src, dst_ref, margin):
        def body(layer, carry):
            down = jnp.maximum(layer - 1, 0)
            up = jnp.minimum(layer + 1, LAY - 1)
            for x in range(-margin, TX + margin):
                j = x + margin + 1
                mid = src(layer, j)
                base = (layer * whole_x + tile * TX + x) * TY
                source = jnp.where(target[0] == base, amount[0], 0.0) + jnp.where(
                    target[1] == base, amount[1], 0.0
                )
                value = (1.0 - OMEGA) * mid + rows(coef_ref, 6, layer, x) * source
                value += rows(coef_ref, 0, layer, x) * src(layer, j - 1)
                value += rows(coef_ref, 1, layer, x) * src(layer, j + 1)
                value += rows(coef_ref, 2, layer, x) * pltpu.roll(mid, 1, 1)
                value += rows(coef_ref, 3, layer, x) * pltpu.roll(mid, TY - 1, 1)
                value += rows(coef_ref, 4, layer, x) * src(down, j)
                value += rows(coef_ref, 5, layer, x) * src(up, j)
                dst_ref[layer, j - 1] = value
            return carry

        lax.fori_loop(0, LAY, body, 0)

    sweep(start, one_ref, 2)
    sweep(lambda layer, j: one_ref[layer, j], two_ref, 1)

    def sense(layer, carry):
        down = jnp.maximum(layer - 1, 0)
        up = jnp.minimum(layer + 1, LAY - 1)
        for x in range(TX):
            j = x + 1
            mid = two_ref[layer, j]
            horiz = rows(grad_ref, 0, layer, x) * (two_ref[layer, j - 1] - mid)
            horiz += rows(grad_ref, 1, layer, x) * (two_ref[layer, j + 1] - mid)
            horiz += rows(grad_ref, 2, layer, x) * (pltpu.roll(mid, 1, 1) - mid)
            horiz += rows(grad_ref, 3, layer, x) * (pltpu.roll(mid, TY - 1, 1) - mid)
            vert = rows(grad_ref, 4, layer, x) * (two_ref[down, j] - mid)
            vert += rows(grad_ref, 5, layer, x) * (two_ref[up, j] - mid)
            chunk = layer * (TX // 2) + x // 2
            half = pl.ds((x % 2) * TY, TY)
            out_ref[chunk, pl.ds(0, OBS), half] = horiz
            out_ref[chunk, pl.ds(OBS, OBS), half] = vert
        return carry

    lax.fori_loop(0, LAY, sense, 0)


def krig_kernel(tile_ref, sens_ref, pilot_ref, med_ref, *rest):
    swap_ref, send_ref, late_ref, own_ref, index_ref, share_ref, total_ref = rest
    tile = tile_ref[0, 0]
    base = (tile - RADIUS) * P_DEV
    chunks = LAY * TX // KX

    for layer in range(LAY):
        index = [pilot_ref[k, layer] - base for k in range(NK)]
        share = [med_ref[layer, 4 + k] for k in range(NK)]
        for k in range(1, NK):
            for j in range(k):
                same = index[j] == index[k]
                share[j] = share[j] + jnp.where(same, share[k], 0.0)
                index[k] = jnp.where(same, -1, index[k])
        for k in range(NK):
            index_ref[k, pl.ds(layer * TX, TX), :] = index[k]
            share_ref[k, pl.ds(layer * TX, TX), :] = share[k]

    iota = lax.broadcasted_iota(I16, (16, TY), 0)
    total_ref[...] = jnp.zeros_like(total_ref)

    def split(value):
        high = value.astype(BF16)
        return high, (value - high.astype(F32)).astype(BF16)

    def body(chunk, carry):
        columns = []
        for s in range(KX):
            row = pl.ds(chunk * KX + s, 1)
            index = []
            high = []
            low = []
            for k in range(NK):
                index.append(jnp.broadcast_to(index_ref[k, row, :], (16, TY)).astype(I16))
                first, second = split(jnp.broadcast_to(share_ref[k, row, :], (16, TY)))
                high.append(first)
                low.append(second)
            uppers = []
            lowers = []
            for i in range(SPAN // 16):
                pilot = iota + I16(16 * i)
                upper = jnp.zeros((16, TY), BF16)
                lower = jnp.zeros((16, TY), BF16)
                for k in range(NK):
                    hit = index[k] == pilot
                    upper = jnp.where(hit, high[k], upper)
                    lower = jnp.where(hit, low[k], lower)
                uppers.append(upper)
                lowers.append(lower)
            columns.append(jnp.concatenate(uppers + lowers, axis=0))
        sens = []
        for q in range(KX // 2):
            sens.append(jnp.concatenate(split(sens_ref[chunk * (KX // 2) + q]), axis=0))
        total_ref[...] += lax.dot_general(
            jnp.concatenate(columns, axis=1),
            jnp.concatenate(sens, axis=1),
            (((1,), (1,)), ((), ())),
            preferred_element_type=F32,
        )
        return carry

    lax.fori_loop(0, chunks, body, 0)

    def piece(o):
        start = pl.multiple_of(o * P_DEV, P_DEV)
        value = total_ref[pl.ds(start, P_DEV), :] + total_ref[pl.ds(SPAN + start, P_DEV), :]
        value = value.T
        return value[: 2 * OBS] + value[2 * OBS :]

    odd = tile % 2
    swap_ref[...] = piece((1 - odd) * 4)
    send_ref[pl.ds(0, 2 * OBS), :] = piece(1 + 2 * odd)
    send_ref[pl.ds(2 * OBS, 2 * OBS), :] = piece(4 * odd)
    late_ref[...] = piece(3 - 2 * odd)
    own_ref[...] = piece(RADIUS)


def swapped(block):
    count = lax.axis_size("grid")
    return lax.ppermute(block, "grid", [(i, i ^ 1) for i in range(count)])


def crossed(block):
    count = lax.axis_size("grid")
    pairs = [(i, i + 1 if i % 2 else i - 1) for i in range(1, count - 1)]
    return lax.ppermute(block, "grid", pairs)


def gathered(block, axis):
    count = lax.axis_size(axis)
    return lax.all_to_all(
        jnp.broadcast_to(block[None], (count,) + block.shape), axis, 0, 0, tiled=False
    )


def shards(
    adjoint_start,
    conductance,
    storage,
    head,
    layer_open,
    krig_weight,
    krig_pilot,
    obs_cell,
    obs_weight,
):
    sds = jax.ShapeDtypeStruct
    tile = jnp.stack([lax.axis_index("grid"), jnp.int32(lax.axis_size("grid"))]).reshape(1, 2)

    own = jnp.concatenate([conductance[:, 0], storage, head, krig_weight[:, 0]], axis=0)
    medium = gathered(own, "obs")

    edge = sds((LAY, HALO, OBS, TY), F32)
    turned, pair, other = pl.pallas_call(
        turn_kernel,
        out_shape=(sds((LAY, TX, OBS, TY), F32), edge, edge),
        in_specs=[SMEM, VMEM],
        out_specs=(VMEM, VMEM, VMEM),
        compiler_params=pltpu.CompilerParams(vmem_limit_bytes=12 * 2**20),
    )(tile, adjoint_start.reshape(OBS * LAY * TX, TY))
    other = crossed(other)
    pair = swapped(pair)

    edge = sds((LAY, 16, TY), F32)
    med_pair, med_other = pl.pallas_call(
        medium_edges_kernel,
        out_shape=(edge, edge),
        in_specs=[SMEM, VMEM, VMEM],
        out_specs=(VMEM, VMEM),
        compiler_params=pltpu.CompilerParams(vmem_limit_bytes=8 * 2**20),
    )(tile, medium, layer_open)
    med_other = crossed(med_other)
    med_pair = swapped(med_pair)

    sens = pl.pallas_call(
        stencil_kernel,
        out_shape=sds((LAY * TX // 2, 2 * OBS, 2 * TY), F32),
        in_specs=[SMEM] + [VMEM] * 9,
        out_specs=VMEM,
        scratch_shapes=[
            pltpu.VMEM((5, LAY, EXT, TY), F32),
            pltpu.VMEM((7, LAY, EXT, TY), F32),
            pltpu.VMEM((6, LAY, EXT, TY), F32),
            pltpu.VMEM((LAY, 2 * HALO, OBS, TY), F32),
            pltpu.VMEM((LAY, TX + 4, OBS, TY), F32),
            pltpu.VMEM((LAY, TX + 2, OBS, TY), F32),
        ],
        compiler_params=pltpu.CompilerParams(vmem_limit_bytes=24 * 2**20),
    )(tile, turned, pair, other, medium, layer_open, med_pair, med_other, obs_cell.T, obs_weight.T)

    piece = sds((2 * OBS, P_DEV), F32)
    swap, send, late, owned = pl.pallas_call(
        krig_kernel,
        out_shape=(piece, sds((4 * OBS, P_DEV), F32), piece, piece),
        in_specs=[SMEM] + [VMEM] * 3,
        out_specs=(VMEM,) * 4,
        scratch_shapes=[
            pltpu.VMEM((NK, LAY * TX, TY), jnp.int32),
            pltpu.VMEM((NK, LAY * TX, TY), F32),
            pltpu.VMEM((2 * SPAN, 4 * OBS), F32),
        ],
        compiler_params=pltpu.CompilerParams(vmem_limit_bytes=28 * 2**20),
    )(tile, sens, krig_pilot, medium)

    half = 2 * OBS
    arrived = crossed(jnp.concatenate([send[:half] + swapped(swap), send[half:]], axis=0))
    owned = owned + arrived[:half] + swapped(late + arrived[half:])
    return owned.reshape(2, OBS, P_DEV)


def solution(mesh):
    return jax.shard_map(
        shards,
        mesh=mesh,
        in_specs=(
            P("obs", None, "grid", None),
            P(None, "obs", "grid", None),
            P("obs", "grid", None),
            P("obs", "grid", None),
            P(None, "grid", None),
            P(None, "obs", "grid", None),
            P(None, None, "grid", None),
            P("obs", None),
            P("obs", None),
        ),
        out_specs=P(None, "obs", "grid"),
        check_vma=False,
    )
```

```python
import jax
import jax.numpy as jnp
from jax import lax
from jax.experimental import pallas as pl
from jax.experimental.pallas import tpu as pltpu
from jax.sharding import PartitionSpec as P


NK = 4
RADIUS = 2
P_DEV = 128
OMEGA = 0.8
LAY = 8
OBS = 32
TX = 16
TY = 128
HALO = 3
SPAN = (2 * RADIUS + 1) * P_DEV
OFF = 8
EXT = 32
KX = 16

F32 = jnp.float32
BF16 = jnp.bfloat16
I16 = jnp.int16
VMEM = pl.BlockSpec(memory_space=pltpu.VMEM)
SMEM = pl.BlockSpec(memory_space=pltpu.SMEM)
HBM = pl.BlockSpec(memory_space=pltpu.HBM)


def spread_kernel(
    cond_ref, storage_ref, head_ref, krig_ref, med_ref, share_ref, own_ref, in_ref, out_ref
):
    parts = (
        (cond_ref.at[:, 0], own_ref.at[pl.ds(0, 2)]),
        (storage_ref, own_ref.at[pl.ds(2, 1)]),
        (head_ref, own_ref.at[pl.ds(3, 1)]),
        (krig_ref.at[:, 0], own_ref.at[pl.ds(4, NK)]),
    )
    loads = [
        pltpu.make_async_copy(part, place, in_ref.at[i]) for i, (part, place) in enumerate(parts)
    ]
    for load in loads:
        load.start()
    for load in loads:
        load.wait()
    stores = []
    for layer in range(LAY):
        for i, ref in enumerate((med_ref, share_ref)):
            stores.append(
                pltpu.make_async_copy(
                    own_ref.at[pl.ds(4 * i, 4)], ref.at[layer], out_ref.at[2 * layer + i]
                )
            )
    for store in stores:
        store.start()
    for store in stores:
        store.wait()


def turn_kernel(tile_ref, adj_ref, turned_ref, pair_ref, other_ref, buf_ref, sem_ref):
    odd = tile_ref[0, 0] % 2
    pair_start = (1 - odd) * (TX - HALO)
    other_start = odd * (TX - HALO)

    def fetch(layer):
        return pltpu.make_async_copy(
            adj_ref.at[:, layer], buf_ref.at[layer], sem_ref.at[layer]
        )

    for layer in range(LAY):
        fetch(layer).start()

    def body(layer, carry):
        fetch(layer).wait()
        rows_ref = buf_ref.at[layer].reshape(OBS * TX, TY)
        for x in range(TX):
            turned_ref[layer, x] = rows_ref[pl.ds(x, OBS, stride=TX), :]
        for j in range(HALO):
            pair_ref[layer, j] = turned_ref[layer, pair_start + j]
            other_ref[layer, j] = turned_ref[layer, other_start + j]
        return carry

    lax.fori_loop(0, LAY, body, 0)


def medium_edges_kernel(tile_ref, med_ref, open_ref, pair_ref, other_ref):
    odd = tile_ref[0, 0] % 2 == 1
    for layer in range(LAY):
        for field in range(5):
            if field < 4:
                tile = med_ref[layer, field]
            else:
                tile = open_ref[layer].astype(F32)
            low = tile[:HALO]
            high = tile[TX - HALO :]
            rows = pl.ds(field * HALO, HALO)
            pair_ref[layer, rows, :] = jnp.where(odd, low, high)
            other_ref[layer, rows, :] = jnp.where(odd, high, low)
        pair_ref[layer, pl.ds(15, 1), :] = jnp.zeros((1, TY), F32)
        other_ref[layer, pl.ds(15, 1), :] = jnp.zeros((1, TY), F32)


def stencil_kernel(
    tile_ref,
    turned_ref,
    pair_ref,
    other_ref,
    med_ref,
    open_ref,
    med_pair_ref,
    med_other_ref,
    cell_ref,
    weight_ref,
    sens_ref,
    ext_ref,
    coef_ref,
    grad_ref,
    halo_ref,
    one_ref,
    two_ref,
    out_ref,
    sem_ref,
):
    tile = tile_ref[0, 0]
    n_tiles = tile_ref[0, 1]
    whole_x = n_tiles * TX
    odd = tile % 2

    row = lax.broadcasted_iota(jnp.int32, (EXT, TY), 0)
    lane = lax.broadcasted_iota(jnp.int32, (EXT, TY), 1)
    global_x = tile * TX + row - OFF
    live = (global_x >= 0) & (global_x < whole_x)
    live_next = (global_x + 1 >= 0) & (global_x + 1 < whole_x)
    both = jnp.where(live & live_next, 1.0, 0.0).astype(F32)
    for layer in range(LAY):
        for field in range(5):
            fill = jnp.ones((OFF, TY), F32)
            ext_ref[field, layer, pl.ds(0, OFF), :] = fill
            ext_ref[field, layer, pl.ds(OFF + TX, OFF), :] = fill
            own = med_ref[layer, field] if field < 4 else open_ref[layer].astype(F32)
            ext_ref[field, layer, pl.ds(OFF, TX), :] = own
            pair = med_pair_ref[layer, pl.ds(field * HALO, HALO), :]
            other = med_other_ref[layer, pl.ds(field * HALO, HALO), :]
            ext_ref[field, layer, pl.ds(OFF - HALO, HALO), :] = jnp.where(odd == 1, pair, other)
            ext_ref[field, layer, pl.ds(OFF + TX, HALO), :] = jnp.where(odd == 1, other, pair)

    def place(layer, carry):
        for j in range(HALO):
            halo_ref[layer, HALO * (1 - odd) + j] = pair_ref[layer, j]
            halo_ref[layer, HALO * odd + j] = other_ref[layer, j]
        return carry

    lax.fori_loop(0, LAY, place, 0)

    def medium(field, layer):
        value = ext_ref[field, layer]
        if field < 3:
            return jnp.where(live, value, 1.0)
        return value

    def below(value):
        return pltpu.roll(value, 1, 0)

    def above(value):
        return pltpu.roll(value, EXT - 1, 0)

    def west(value):
        return pltpu.roll(value, 1, 1)

    def east(value):
        return pltpu.roll(value, TY - 1, 1)

    has_west = jnp.where(lane > 0, 1.0, 0.0).astype(F32)
    has_east = jnp.where(lane < TY - 1, 1.0, 0.0).astype(F32)
    before = below(both)

    def faces(mine, other):
        inv = 1.0 / (mine + other)
        face = 2.0 * mine * other * inv
        return face, face * other * inv

    for layer in range(LAY):
        k = medium(0, layer)
        kv = medium(1, layer)
        head = medium(3, layer)
        fxm, gxm = faces(k, below(k))
        fxp, gxp = faces(k, above(k))
        fym, gym = faces(k, west(k))
        fyp, gyp = faces(k, east(k))
        fxm = fxm * before
        fxp = fxp * both
        fym = fym * has_west
        fyp = fyp * has_east
        diag = medium(2, layer) + fxm + fxp + fym + fyp
        zero = jnp.zeros((EXT, TY), F32)
        fzm = fzp = gzm = gzp = zero
        if layer > 0:
            fzm, gzm = faces(kv, medium(1, layer - 1))
            gate = ext_ref[4, layer - 1]
            fzm = fzm * gate
            gzm = gzm * gate * (head - medium(3, layer - 1))
        if layer < LAY - 1:
            fzp, gzp = faces(kv, medium(1, layer + 1))
            gate = ext_ref[4, layer]
            fzp = fzp * gate
            gzp = gzp * gate * (head - medium(3, layer + 1))
        diag = diag + fzm + fzp
        scale = OMEGA / diag
        for n, value in enumerate((fxm, fxp, fym, fyp, fzm, fzp)):
            coef_ref[n, layer] = value * scale
        coef_ref[6, layer] = scale
        grad_ref[0, layer] = gxm * before * (head - below(head))
        grad_ref[1, layer] = gxp * both * (head - above(head))
        grad_ref[2, layer] = gym * has_west * (head - west(head))
        grad_ref[3, layer] = gyp * has_east * (head - east(head))
        grad_ref[4, layer] = gzm
        grad_ref[5, layer] = gzp

    lanes = lax.broadcasted_iota(jnp.int32, (OBS, TY), 1)
    eye = lax.broadcasted_iota(jnp.int32, (OBS, OBS), 0) == lax.broadcasted_iota(
        jnp.int32, (OBS, OBS), 1
    )

    def column(row):
        square = jnp.where(eye, jnp.broadcast_to(row, (OBS, OBS)), 0.0)
        return jnp.broadcast_to(jnp.sum(square, axis=1, keepdims=True), (OBS, TY))

    target = [
        column(cell_ref[pl.ds(m, 1), :].astype(F32)).astype(jnp.int32) - lanes for m in range(2)
    ]
    amount = [column(weight_ref[pl.ds(m, 1), :]) for m in range(2)]

    def rows(ref, n, layer, x):
        return jnp.broadcast_to(ref[n, layer, pl.ds(x + OFF, 1), :], (OBS, TY))

    def start(layer, j):
        if j < HALO:
            return halo_ref[layer, j]
        if j < HALO + TX:
            return turned_ref[layer, j - HALO]
        return halo_ref[layer, j - TX]

    def sweep(src, dst_ref, margin):
        def body(layer, carry):
            down = jnp.maximum(layer - 1, 0)
            up = jnp.minimum(layer + 1, LAY - 1)
            for x in range(-margin, TX + margin):
                j = x + margin + 1
                mid = src(layer, j)
                base = (layer * whole_x + tile * TX + x) * TY
                source = jnp.where(target[0] == base, amount[0], 0.0) + jnp.where(
                    target[1] == base, amount[1], 0.0
                )
                value = (1.0 - OMEGA) * mid + rows(coef_ref, 6, layer, x) * source
                value += rows(coef_ref, 0, layer, x) * src(layer, j - 1)
                value += rows(coef_ref, 1, layer, x) * src(layer, j + 1)
                value += rows(coef_ref, 2, layer, x) * pltpu.roll(mid, 1, 1)
                value += rows(coef_ref, 3, layer, x) * pltpu.roll(mid, TY - 1, 1)
                value += rows(coef_ref, 4, layer, x) * src(down, j)
                value += rows(coef_ref, 5, layer, x) * src(up, j)
                dst_ref[layer, j - 1] = value
            return carry

        lax.fori_loop(0, LAY, body, 0)

    sweep(start, one_ref, 2)
    sweep(lambda layer, j: one_ref[layer, j], two_ref, 1)

    def store(layer):
        part = pl.ds(layer * (TX // 2), TX // 2)
        return pltpu.make_async_copy(out_ref.at[part], sens_ref.at[part], sem_ref.at[layer])

    def sense(layer, carry):
        down = jnp.maximum(layer - 1, 0)
        up = jnp.minimum(layer + 1, LAY - 1)
        for x in range(TX):
            j = x + 1
            mid = two_ref[layer, j]
            horiz = rows(grad_ref, 0, layer, x) * (two_ref[layer, j - 1] - mid)
            horiz += rows(grad_ref, 1, layer, x) * (two_ref[layer, j + 1] - mid)
            horiz += rows(grad_ref, 2, layer, x) * (pltpu.roll(mid, 1, 1) - mid)
            horiz += rows(grad_ref, 3, layer, x) * (pltpu.roll(mid, TY - 1, 1) - mid)
            vert = rows(grad_ref, 4, layer, x) * (two_ref[down, j] - mid)
            vert += rows(grad_ref, 5, layer, x) * (two_ref[up, j] - mid)
            chunk = layer * (TX // 2) + x // 2
            half = pl.ds((x % 2) * TY, TY)
            out_ref[chunk, pl.ds(0, OBS), half] = horiz
            out_ref[chunk, pl.ds(OBS, OBS), half] = vert
        store(layer).start()
        return carry

    lax.fori_loop(0, LAY, sense, 0)
    for layer in range(LAY):
        store(layer).wait()


def krig_kernel(tile_ref, far_ref, pilot_ref, weight_ref, *rest):
    swap_ref, send_ref, late_ref, own_ref, index_ref, share_ref, total_ref, sens_ref, sem_ref = rest

    def fetch(chunk):
        part = pl.ds(chunk * (KX // 2), KX // 2)
        return pltpu.make_async_copy(far_ref.at[part], sens_ref.at[part], sem_ref.at[chunk])

    for chunk in range(LAY * TX // KX):
        fetch(chunk).start()
    tile = tile_ref[0, 0]
    base = (tile - RADIUS) * P_DEV
    chunks = LAY * TX // KX

    for layer in range(LAY):
        index = [pilot_ref[k, layer] - base for k in range(NK)]
        share = [weight_ref[layer, k] for k in range(NK)]
        for k in range(1, NK):
            for j in range(k):
                same = index[j] == index[k]
                share[j] = share[j] + jnp.where(same, share[k], 0.0)
                index[k] = jnp.where(same, -1, index[k])
        for k in range(NK):
            index_ref[k, pl.ds(layer * TX, TX), :] = index[k]
            share_ref[k, pl.ds(layer * TX, TX), :] = share[k]

    iota = lax.broadcasted_iota(I16, (16, TY), 0)
    total_ref[...] = jnp.zeros_like(total_ref)

    def split(value):
        high = value.astype(BF16)
        return high, (value - high.astype(F32)).astype(BF16)

    def body(chunk, carry):
        columns = []
        for s in range(KX):
            row = pl.ds(chunk * KX + s, 1)
            index = []
            high = []
            low = []
            for k in range(NK):
                index.append(jnp.broadcast_to(index_ref[k, row, :], (16, TY)).astype(I16))
                first, second = split(jnp.broadcast_to(share_ref[k, row, :], (16, TY)))
                high.append(first)
                low.append(second)
            uppers = []
            lowers = []
            for i in range(SPAN // 16):
                pilot = iota + I16(16 * i)
                upper = jnp.zeros((16, TY), BF16)
                lower = jnp.zeros((16, TY), BF16)
                for k in range(NK):
                    hit = index[k] == pilot
                    upper = jnp.where(hit, high[k], upper)
                    lower = jnp.where(hit, low[k], lower)
                uppers.append(upper)
                lowers.append(lower)
            columns.append(jnp.concatenate(uppers + lowers, axis=0))
        fetch(chunk).wait()
        sens = []
        for q in range(KX // 2):
            sens.append(jnp.concatenate(split(sens_ref[chunk * (KX // 2) + q]), axis=0))
        total_ref[...] += lax.dot_general(
            jnp.concatenate(columns, axis=1),
            jnp.concatenate(sens, axis=1),
            (((1,), (1,)), ((), ())),
            preferred_element_type=F32,
        )
        return carry

    lax.fori_loop(0, chunks, body, 0)

    def piece(o):
        start = pl.multiple_of(o * P_DEV, P_DEV)
        value = total_ref[pl.ds(start, P_DEV), :] + total_ref[pl.ds(SPAN + start, P_DEV), :]
        value = value.T
        return value[: 2 * OBS] + value[2 * OBS :]

    odd = tile % 2
    swap_ref[...] = piece((1 - odd) * 4)
    send_ref[pl.ds(0, 2 * OBS), :] = piece(1 + 2 * odd)
    send_ref[pl.ds(2 * OBS, 2 * OBS), :] = piece(4 * odd)
    late_ref[...] = piece(3 - 2 * odd)
    own_ref[...] = piece(RADIUS)


def in_hbm(array):
    return pltpu.with_memory_space_constraint(array, pltpu.HBM)


def swapped(block):
    count = lax.axis_size("grid")
    return lax.ppermute(block, "grid", [(i, i ^ 1) for i in range(count)])


def crossed(block):
    count = lax.axis_size("grid")
    pairs = [(i, i + 1 if i % 2 else i - 1) for i in range(1, count - 1)]
    return lax.ppermute(block, "grid", pairs)


def gathered(copies, axis):
    return lax.all_to_all(copies, axis, 0, 0, tiled=False)


def local(
    adjoint_start,
    conductance,
    storage,
    head,
    layer_open,
    krig_weight,
    krig_pilot,
    obs_cell,
    obs_weight,
):
    sds = jax.ShapeDtypeStruct
    tile = jnp.stack([lax.axis_index("grid"), jnp.int32(lax.axis_size("grid"))]).reshape(1, 2)

    copies = pltpu.HBM((LAY, 4, TX, TY), F32)
    med_copies, share_copies = pl.pallas_call(
        spread_kernel,
        out_shape=(copies, copies),
        in_specs=[HBM] * 4,
        out_specs=(HBM, HBM),
        scratch_shapes=[
            pltpu.VMEM((4 + NK, TX, TY), F32),
            pltpu.SemaphoreType.DMA((4,)),
            pltpu.SemaphoreType.DMA((2 * LAY,)),
        ],
        compiler_params=pltpu.CompilerParams(vmem_limit_bytes=4 * 2**20),
    )(*map(in_hbm, (conductance, storage, head, krig_weight)))
    medium = gathered(med_copies, "obs")

    edge = sds((LAY, HALO, OBS, TY), F32)
    turned, pair, other = pl.pallas_call(
        turn_kernel,
        out_shape=(sds((LAY, TX, OBS, TY), F32), edge, edge),
        in_specs=[SMEM, HBM],
        out_specs=(VMEM, VMEM, VMEM),
        scratch_shapes=[
            pltpu.VMEM((LAY, OBS, TX, TY), F32),
            pltpu.SemaphoreType.DMA((LAY,)),
        ],
        compiler_params=pltpu.CompilerParams(vmem_limit_bytes=12 * 2**20),
    )(tile, in_hbm(adjoint_start))
    other = crossed(other)
    pair = swapped(pair)

    edge = sds((LAY, 16, TY), F32)
    med_pair, med_other = pl.pallas_call(
        medium_edges_kernel,
        out_shape=(edge, edge),
        in_specs=[SMEM, VMEM, VMEM],
        out_specs=(VMEM, VMEM),
        compiler_params=pltpu.CompilerParams(vmem_limit_bytes=8 * 2**20),
    )(tile, medium, layer_open)
    med_other = crossed(med_other)
    med_pair = swapped(med_pair)
    share = gathered(share_copies, "obs")

    sens = pl.pallas_call(
        stencil_kernel,
        out_shape=pltpu.HBM((LAY * TX // 2, 2 * OBS, 2 * TY), F32),
        in_specs=[SMEM] + [VMEM] * 9,
        out_specs=HBM,
        scratch_shapes=[
            pltpu.VMEM((5, LAY, EXT, TY), F32),
            pltpu.VMEM((7, LAY, EXT, TY), F32),
            pltpu.VMEM((6, LAY, EXT, TY), F32),
            pltpu.VMEM((LAY, 2 * HALO, OBS, TY), F32),
            pltpu.VMEM((LAY, TX + 4, OBS, TY), F32),
            pltpu.VMEM((LAY, TX + 2, OBS, TY), F32),
            pltpu.VMEM((LAY * TX // 2, 2 * OBS, 2 * TY), F32),
            pltpu.SemaphoreType.DMA((LAY,)),
        ],
        compiler_params=pltpu.CompilerParams(vmem_limit_bytes=24 * 2**20),
    )(tile, turned, pair, other, medium, layer_open, med_pair, med_other, obs_cell.T, obs_weight.T)

    piece = sds((2 * OBS, P_DEV), F32)
    swap, send, late, owned = pl.pallas_call(
        krig_kernel,
        out_shape=(piece, sds((4 * OBS, P_DEV), F32), piece, piece),
        in_specs=[SMEM, HBM, VMEM, VMEM],
        out_specs=(VMEM,) * 4,
        scratch_shapes=[
            pltpu.VMEM((NK, LAY * TX, TY), jnp.int32),
            pltpu.VMEM((NK, LAY * TX, TY), F32),
            pltpu.VMEM((2 * SPAN, 4 * OBS), F32),
            pltpu.VMEM((LAY * TX // 2, 2 * OBS, 2 * TY), F32),
            pltpu.SemaphoreType.DMA((LAY * TX // KX,)),
        ],
        compiler_params=pltpu.CompilerParams(vmem_limit_bytes=24 * 2**20),
    )(tile, in_hbm(sens), krig_pilot, share)

    half = 2 * OBS
    arrived = crossed(jnp.concatenate([send[:half] + swapped(swap), send[half:]], axis=0))
    owned = owned + arrived[:half] + swapped(late + arrived[half:])
    return owned.reshape(2, OBS, P_DEV)


def solution(mesh):
    return jax.shard_map(
        local,
        mesh=mesh,
        in_specs=(
            P("obs", None, "grid", None),
            P(None, "obs", "grid", None),
            P("obs", "grid", None),
            P("obs", "grid", None),
            P(None, "grid", None),
            P(None, "obs", "grid", None),
            P(None, None, "grid", None),
            P("obs", None),
            P("obs", None),
        ),
        out_specs=P(None, "obs", "grid"),
        check_vma=False,
    )
```

```python
import jax
import jax.numpy as jnp
from jax import lax
from jax.experimental import pallas as pl
from jax.experimental.pallas import tpu as pltpu
from jax.sharding import PartitionSpec as P


NK = 4
RADIUS = 2
P_DEV = 128
OMEGA = 0.8
LAY = 8
OBS = 32
TX = 16
TY = 128
HALO = 3
SPAN = (2 * RADIUS + 1) * P_DEV
OFF = 8
EXT = 32
KX = 16

F32 = jnp.float32
BF16 = jnp.bfloat16
I16 = jnp.int16
VMEM = pl.BlockSpec(memory_space=pltpu.VMEM)
SMEM = pl.BlockSpec(memory_space=pltpu.SMEM)
HBM = pl.BlockSpec(memory_space=pltpu.HBM)


def spread_kernel(cond_ref, storage_ref, head_ref, krig_ref, med_ref, own_ref, in_ref, out_ref):
    parts = (
        (cond_ref.at[:, 0], own_ref.at[pl.ds(0, 2)]),
        (storage_ref, own_ref.at[pl.ds(2, 1)]),
        (head_ref, own_ref.at[pl.ds(3, 1)]),
        (krig_ref.at[:, 0], own_ref.at[pl.ds(4, NK)]),
    )
    loads = [
        pltpu.make_async_copy(part, place, in_ref.at[i]) for i, (part, place) in enumerate(parts)
    ]
    for load in loads:
        load.start()
    for load in loads:
        load.wait()
    stores = [
        pltpu.make_async_copy(own_ref, med_ref.at[layer], out_ref.at[layer])
        for layer in range(LAY)
    ]
    for store in stores:
        store.start()
    for store in stores:
        store.wait()


def turn_kernel(tile_ref, adj_ref, turned_ref, pair_ref, other_ref, buf_ref, sem_ref):
    odd = tile_ref[0, 0] % 2
    pair_start = (1 - odd) * (TX - HALO)
    other_start = odd * (TX - HALO)

    def fetch(layer):
        return pltpu.make_async_copy(
            adj_ref.at[:, layer], buf_ref.at[layer], sem_ref.at[layer]
        )

    for layer in range(LAY):
        fetch(layer).start()

    def body(layer, carry):
        fetch(layer).wait()
        rows_ref = buf_ref.at[layer].reshape(OBS * TX, TY)
        for x in range(TX):
            turned_ref[layer, x] = rows_ref[pl.ds(x, OBS, stride=TX), :]
        for j in range(HALO):
            pair_ref[layer, j] = turned_ref[layer, pair_start + j]
            other_ref[layer, j] = turned_ref[layer, other_start + j]
        return carry

    lax.fori_loop(0, LAY, body, 0)


def medium_edges_kernel(tile_ref, med_ref, open_ref, pair_ref, other_ref):
    odd = tile_ref[0, 0] % 2 == 1
    for layer in range(LAY):
        for field in range(5):
            if field < 4:
                tile = med_ref[layer, field]
            else:
                tile = open_ref[layer].astype(F32)
            low = tile[:HALO]
            high = tile[TX - HALO :]
            rows = pl.ds(field * HALO, HALO)
            pair_ref[layer, rows, :] = jnp.where(odd, low, high)
            other_ref[layer, rows, :] = jnp.where(odd, high, low)
        pair_ref[layer, pl.ds(15, 1), :] = jnp.zeros((1, TY), F32)
        other_ref[layer, pl.ds(15, 1), :] = jnp.zeros((1, TY), F32)


def stencil_kernel(
    tile_ref,
    turned_ref,
    pair_ref,
    other_ref,
    med_ref,
    open_ref,
    med_pair_ref,
    med_other_ref,
    cell_ref,
    weight_ref,
    out_ref,
    ext_ref,
    coef_ref,
    grad_ref,
    halo_ref,
    one_ref,
    two_ref,
):
    tile = tile_ref[0, 0]
    n_tiles = tile_ref[0, 1]
    whole_x = n_tiles * TX
    odd = tile % 2

    row = lax.broadcasted_iota(jnp.int32, (EXT, TY), 0)
    lane = lax.broadcasted_iota(jnp.int32, (EXT, TY), 1)
    global_x = tile * TX + row - OFF
    live = (global_x >= 0) & (global_x < whole_x)
    live_next = (global_x + 1 >= 0) & (global_x + 1 < whole_x)
    both = jnp.where(live & live_next, 1.0, 0.0).astype(F32)
    for layer in range(LAY):
        for field in range(5):
            fill = jnp.ones((OFF, TY), F32)
            ext_ref[field, layer, pl.ds(0, OFF), :] = fill
            ext_ref[field, layer, pl.ds(OFF + TX, OFF), :] = fill
            own = med_ref[layer, field] if field < 4 else open_ref[layer].astype(F32)
            ext_ref[field, layer, pl.ds(OFF, TX), :] = own
            pair = med_pair_ref[layer, pl.ds(field * HALO, HALO), :]
            other = med_other_ref[layer, pl.ds(field * HALO, HALO), :]
            ext_ref[field, layer, pl.ds(OFF - HALO, HALO), :] = jnp.where(odd == 1, pair, other)
            ext_ref[field, layer, pl.ds(OFF + TX, HALO), :] = jnp.where(odd == 1, other, pair)

    def place(layer, carry):
        for j in range(HALO):
            halo_ref[layer, HALO * (1 - odd) + j] = pair_ref[layer, j]
            halo_ref[layer, HALO * odd + j] = other_ref[layer, j]
        return carry

    lax.fori_loop(0, LAY, place, 0)

    def medium(field, layer):
        value = ext_ref[field, layer]
        if field < 3:
            return jnp.where(live, value, 1.0)
        return value

    def below(value):
        return pltpu.roll(value, 1, 0)

    def above(value):
        return pltpu.roll(value, EXT - 1, 0)

    def west(value):
        return pltpu.roll(value, 1, 1)

    def east(value):
        return pltpu.roll(value, TY - 1, 1)

    has_west = jnp.where(lane > 0, 1.0, 0.0).astype(F32)
    has_east = jnp.where(lane < TY - 1, 1.0, 0.0).astype(F32)
    before = below(both)

    def faces(mine, other):
        inv = 1.0 / (mine + other)
        face = 2.0 * mine * other * inv
        return face, face * other * inv

    for layer in range(LAY):
        k = medium(0, layer)
        kv = medium(1, layer)
        head = medium(3, layer)
        fxm, gxm = faces(k, below(k))
        fxp, gxp = faces(k, above(k))
        fym, gym = faces(k, west(k))
        fyp, gyp = faces(k, east(k))
        fxm = fxm * before
        fxp = fxp * both
        fym = fym * has_west
        fyp = fyp * has_east
        diag = medium(2, layer) + fxm + fxp + fym + fyp
        zero = jnp.zeros((EXT, TY), F32)
        fzm = fzp = gzm = gzp = zero
        if layer > 0:
            fzm, gzm = faces(kv, medium(1, layer - 1))
            gate = ext_ref[4, layer - 1]
            fzm = fzm * gate
            gzm = gzm * gate * (head - medium(3, layer - 1))
        if layer < LAY - 1:
            fzp, gzp = faces(kv, medium(1, layer + 1))
            gate = ext_ref[4, layer]
            fzp = fzp * gate
            gzp = gzp * gate * (head - medium(3, layer + 1))
        diag = diag + fzm + fzp
        scale = OMEGA / diag
        for n, value in enumerate((fxm, fxp, fym, fyp, fzm, fzp)):
            coef_ref[n, layer] = value * scale
        coef_ref[6, layer] = scale
        grad_ref[0, layer] = gxm * before * (head - below(head))
        grad_ref[1, layer] = gxp * both * (head - above(head))
        grad_ref[2, layer] = gym * has_west * (head - west(head))
        grad_ref[3, layer] = gyp * has_east * (head - east(head))
        grad_ref[4, layer] = gzm
        grad_ref[5, layer] = gzp

    lanes = lax.broadcasted_iota(jnp.int32, (OBS, TY), 1)
    eye = lax.broadcasted_iota(jnp.int32, (OBS, OBS), 0) == lax.broadcasted_iota(
        jnp.int32, (OBS, OBS), 1
    )

    def column(row):
        square = jnp.where(eye, jnp.broadcast_to(row, (OBS, OBS)), 0.0)
        return jnp.broadcast_to(jnp.sum(square, axis=1, keepdims=True), (OBS, TY))

    target = [
        column(cell_ref[pl.ds(m, 1), :].astype(F32)).astype(jnp.int32) - lanes for m in range(2)
    ]
    amount = [column(weight_ref[pl.ds(m, 1), :]) for m in range(2)]

    def rows(ref, n, layer, x):
        return jnp.broadcast_to(ref[n, layer, pl.ds(x + OFF, 1), :], (OBS, TY))

    def start(layer, j):
        if j < HALO:
            return halo_ref[layer, j]
        if j < HALO + TX:
            return turned_ref[layer, j - HALO]
        return halo_ref[layer, j - TX]

    def sweep(src, dst_ref, margin):
        def body(layer, carry):
            down = jnp.maximum(layer - 1, 0)
            up = jnp.minimum(layer + 1, LAY - 1)
            for x in range(-margin, TX + margin):
                j = x + margin + 1
                mid = src(layer, j)
                base = (layer * whole_x + tile * TX + x) * TY
                source = jnp.where(target[0] == base, amount[0], 0.0) + jnp.where(
                    target[1] == base, amount[1], 0.0
                )
                value = (1.0 - OMEGA) * mid + rows(coef_ref, 6, layer, x) * source
                value += rows(coef_ref, 0, layer, x) * src(layer, j - 1)
                value += rows(coef_ref, 1, layer, x) * src(layer, j + 1)
                value += rows(coef_ref, 2, layer, x) * pltpu.roll(mid, 1, 1)
                value += rows(coef_ref, 3, layer, x) * pltpu.roll(mid, TY - 1, 1)
                value += rows(coef_ref, 4, layer, x) * src(down, j)
                value += rows(coef_ref, 5, layer, x) * src(up, j)
                dst_ref[layer, j - 1] = value
            return carry

        lax.fori_loop(0, LAY, body, 0)

    sweep(start, one_ref, 2)
    sweep(lambda layer, j: one_ref[layer, j], two_ref, 1)

    def sense(layer, carry):
        down = jnp.maximum(layer - 1, 0)
        up = jnp.minimum(layer + 1, LAY - 1)
        for x in range(TX):
            j = x + 1
            mid = two_ref[layer, j]
            horiz = rows(grad_ref, 0, layer, x) * (two_ref[layer, j - 1] - mid)
            horiz += rows(grad_ref, 1, layer, x) * (two_ref[layer, j + 1] - mid)
            horiz += rows(grad_ref, 2, layer, x) * (pltpu.roll(mid, 1, 1) - mid)
            horiz += rows(grad_ref, 3, layer, x) * (pltpu.roll(mid, TY - 1, 1) - mid)
            vert = rows(grad_ref, 4, layer, x) * (two_ref[down, j] - mid)
            vert += rows(grad_ref, 5, layer, x) * (two_ref[up, j] - mid)
            chunk = layer * (TX // 2) + x // 2
            half = pl.ds((x % 2) * TY, TY)
            out_ref[chunk, pl.ds(0, OBS), half] = horiz
            out_ref[chunk, pl.ds(OBS, OBS), half] = vert
        return carry

    lax.fori_loop(0, LAY, sense, 0)


def krig_kernel(tile_ref, sens_ref, pilot_ref, med_ref, *rest):
    swap_ref, send_ref, late_ref, own_ref, index_ref, share_ref, total_ref = rest
    tile = tile_ref[0, 0]
    base = (tile - RADIUS) * P_DEV
    chunks = LAY * TX // KX

    for layer in range(LAY):
        index = [pilot_ref[k, layer] - base for k in range(NK)]
        share = [med_ref[layer, 4 + k] for k in range(NK)]
        for k in range(1, NK):
            for j in range(k):
                same = index[j] == index[k]
                share[j] = share[j] + jnp.where(same, share[k], 0.0)
                index[k] = jnp.where(same, -1, index[k])
        for k in range(NK):
            index_ref[k, pl.ds(layer * TX, TX), :] = index[k]
            share_ref[k, pl.ds(layer * TX, TX), :] = share[k]

    iota = lax.broadcasted_iota(I16, (16, TY), 0)
    total_ref[...] = jnp.zeros_like(total_ref)

    def split(value):
        high = value.astype(BF16)
        return high, (value - high.astype(F32)).astype(BF16)

    def body(chunk, carry):
        columns = []
        for s in range(KX):
            row = pl.ds(chunk * KX + s, 1)
            index = []
            high = []
            low = []
            for k in range(NK):
                index.append(jnp.broadcast_to(index_ref[k, row, :], (16, TY)).astype(I16))
                first, second = split(jnp.broadcast_to(share_ref[k, row, :], (16, TY)))
                high.append(first)
                low.append(second)
            uppers = []
            lowers = []
            for i in range(SPAN // 16):
                pilot = iota + I16(16 * i)
                upper = jnp.zeros((16, TY), BF16)
                lower = jnp.zeros((16, TY), BF16)
                for k in range(NK):
                    hit = index[k] == pilot
                    upper = jnp.where(hit, high[k], upper)
                    lower = jnp.where(hit, low[k], lower)
                uppers.append(upper)
                lowers.append(lower)
            columns.append(jnp.concatenate(uppers + lowers, axis=0))
        sens = []
        for q in range(KX // 2):
            sens.append(jnp.concatenate(split(sens_ref[chunk * (KX // 2) + q]), axis=0))
        total_ref[...] += lax.dot_general(
            jnp.concatenate(columns, axis=1),
            jnp.concatenate(sens, axis=1),
            (((1,), (1,)), ((), ())),
            preferred_element_type=F32,
        )
        return carry

    lax.fori_loop(0, chunks, body, 0)

    def piece(o):
        start = pl.multiple_of(o * P_DEV, P_DEV)
        value = total_ref[pl.ds(start, P_DEV), :] + total_ref[pl.ds(SPAN + start, P_DEV), :]
        value = value.T
        return value[: 2 * OBS] + value[2 * OBS :]

    odd = tile % 2
    swap_ref[...] = piece((1 - odd) * 4)
    send_ref[pl.ds(0, 2 * OBS), :] = piece(1 + 2 * odd)
    send_ref[pl.ds(2 * OBS, 2 * OBS), :] = piece(4 * odd)
    late_ref[...] = piece(3 - 2 * odd)
    own_ref[...] = piece(RADIUS)


def in_hbm(array):
    return pltpu.with_memory_space_constraint(array, pltpu.HBM)


def swapped(block):
    count = lax.axis_size("grid")
    return lax.ppermute(block, "grid", [(i, i ^ 1) for i in range(count)])


def crossed(block):
    count = lax.axis_size("grid")
    pairs = [(i, i + 1 if i % 2 else i - 1) for i in range(1, count - 1)]
    return lax.ppermute(block, "grid", pairs)


def gathered(copies, axis):
    return lax.all_to_all(copies, axis, 0, 0, tiled=False)


def local(
    adjoint_start,
    conductance,
    storage,
    head,
    layer_open,
    krig_weight,
    krig_pilot,
    obs_cell,
    obs_weight,
):
    sds = jax.ShapeDtypeStruct
    tile = jnp.stack([lax.axis_index("grid"), jnp.int32(lax.axis_size("grid"))]).reshape(1, 2)

    copies = pltpu.HBM((LAY, 4 + NK, TX, TY), F32)
    copies = pl.pallas_call(
        spread_kernel,
        out_shape=copies,
        in_specs=[HBM] * 4,
        out_specs=HBM,
        scratch_shapes=[
            pltpu.VMEM((4 + NK, TX, TY), F32),
            pltpu.SemaphoreType.DMA((4,)),
            pltpu.SemaphoreType.DMA((LAY,)),
        ],
        compiler_params=pltpu.CompilerParams(vmem_limit_bytes=4 * 2**20),
    )(*map(in_hbm, (conductance, storage, head, krig_weight)))
    medium = gathered(copies, "obs")

    edge = sds((LAY, HALO, OBS, TY), F32)
    turned, pair, other = pl.pallas_call(
        turn_kernel,
        out_shape=(sds((LAY, TX, OBS, TY), F32), edge, edge),
        in_specs=[SMEM, HBM],
        out_specs=(VMEM, VMEM, VMEM),
        scratch_shapes=[
            pltpu.VMEM((LAY, OBS, TX, TY), F32),
            pltpu.SemaphoreType.DMA((LAY,)),
        ],
        compiler_params=pltpu.CompilerParams(vmem_limit_bytes=12 * 2**20),
    )(tile, in_hbm(adjoint_start))
    other = crossed(other)
    pair = swapped(pair)

    edge = sds((LAY, 16, TY), F32)
    med_pair, med_other = pl.pallas_call(
        medium_edges_kernel,
        out_shape=(edge, edge),
        in_specs=[SMEM, VMEM, VMEM],
        out_specs=(VMEM, VMEM),
        compiler_params=pltpu.CompilerParams(vmem_limit_bytes=8 * 2**20),
    )(tile, medium, layer_open)
    med_other = crossed(med_other)
    med_pair = swapped(med_pair)

    sens = pl.pallas_call(
        stencil_kernel,
        out_shape=sds((LAY * TX // 2, 2 * OBS, 2 * TY), F32),
        in_specs=[SMEM] + [VMEM] * 9,
        out_specs=VMEM,
        scratch_shapes=[
            pltpu.VMEM((5, LAY, EXT, TY), F32),
            pltpu.VMEM((7, LAY, EXT, TY), F32),
            pltpu.VMEM((6, LAY, EXT, TY), F32),
            pltpu.VMEM((LAY, 2 * HALO, OBS, TY), F32),
            pltpu.VMEM((LAY, TX + 4, OBS, TY), F32),
            pltpu.VMEM((LAY, TX + 2, OBS, TY), F32),
        ],
        compiler_params=pltpu.CompilerParams(vmem_limit_bytes=24 * 2**20),
    )(
        tile,
        turned,
        pair,
        other,
        medium,
        layer_open,
        med_pair,
        med_other,
        obs_cell.T,
        obs_weight.T,
    )

    piece = sds((2 * OBS, P_DEV), F32)
    swap, send, late, owned = pl.pallas_call(
        krig_kernel,
        out_shape=(piece, sds((4 * OBS, P_DEV), F32), piece, piece),
        in_specs=[SMEM] + [VMEM] * 3,
        out_specs=(VMEM,) * 4,
        scratch_shapes=[
            pltpu.VMEM((NK, LAY * TX, TY), jnp.int32),
            pltpu.VMEM((NK, LAY * TX, TY), F32),
            pltpu.VMEM((2 * SPAN, 4 * OBS), F32),
        ],
        compiler_params=pltpu.CompilerParams(vmem_limit_bytes=24 * 2**20),
    )(tile, sens, krig_pilot, medium)

    half = 2 * OBS
    arrived = crossed(jnp.concatenate([send[:half] + swapped(swap), send[half:]], axis=0))
    owned = owned + arrived[:half] + swapped(late + arrived[half:])
    return owned.reshape(2, OBS, P_DEV)


def solution(mesh):
    return jax.shard_map(
        local,
        mesh=mesh,
        in_specs=(
            P("obs", None, "grid", None),
            P(None, "obs", "grid", None),
            P("obs", "grid", None),
            P("obs", "grid", None),
            P(None, "grid", None),
            P(None, "obs", "grid", None),
            P(None, None, "grid", None),
            P("obs", None),
            P("obs", None),
        ),
        out_specs=P(None, "obs", "grid"),
        check_vma=False,
    )
```

```python
import jax
import jax.numpy as jnp
from jax import lax
from jax.experimental import pallas as pl
from jax.experimental.pallas import tpu as pltpu
from jax.sharding import PartitionSpec as P


NK = 4
RADIUS = 2
P_DEV = 128
OMEGA = 0.8
LAY = 8
OBS = 32
TX = 16
TY = 128
HALO = 3
SPAN = (2 * RADIUS + 1) * P_DEV
OFF = 8
EXT = 32
KX = 16

F32 = jnp.float32
BF16 = jnp.bfloat16
I16 = jnp.int16
VMEM = pl.BlockSpec(memory_space=pltpu.VMEM)
SMEM = pl.BlockSpec(memory_space=pltpu.SMEM)
HBM = pl.BlockSpec(memory_space=pltpu.HBM)


def spread_kernel(cond_ref, storage_ref, head_ref, krig_ref, med_ref, sem_ref):
    parts = (
        (cond_ref.at[:, 0], 0, 2),
        (storage_ref, 2, 1),
        (head_ref, 3, 1),
        (krig_ref.at[:, 0], 4, NK),
    )
    copies = []
    for layer in range(LAY):
        for i, (part, first, count) in enumerate(parts):
            copies.append(
                pltpu.make_async_copy(
                    part,
                    med_ref.at[layer, pl.ds(first, count)],
                    sem_ref.at[len(parts) * layer + i],
                )
            )
    for copy in copies:
        copy.start()
    for copy in copies:
        copy.wait()


def turn_kernel(tile_ref, adj_ref, turned_ref, pair_ref, other_ref, buf_ref, sem_ref):
    odd = tile_ref[0, 0] % 2
    pair_start = (1 - odd) * (TX - HALO)
    other_start = odd * (TX - HALO)

    def fetch(layer):
        return pltpu.make_async_copy(
            adj_ref.at[:, layer], buf_ref.at[layer], sem_ref.at[layer]
        )

    for layer in range(LAY):
        fetch(layer).start()

    def body(layer, carry):
        fetch(layer).wait()
        rows_ref = buf_ref.at[layer].reshape(OBS * TX, TY)
        for x in range(TX):
            turned_ref[layer, x] = rows_ref[pl.ds(x, OBS, stride=TX), :]
        for j in range(HALO):
            pair_ref[layer, j] = turned_ref[layer, pair_start + j]
            other_ref[layer, j] = turned_ref[layer, other_start + j]
        return carry

    lax.fori_loop(0, LAY, body, 0)


def medium_edges_kernel(tile_ref, med_ref, open_ref, pair_ref, other_ref):
    odd = tile_ref[0, 0] % 2 == 1
    for layer in range(LAY):
        for field in range(5):
            if field < 4:
                tile = med_ref[layer, field]
            else:
                tile = open_ref[layer].astype(F32)
            low = tile[:HALO]
            high = tile[TX - HALO :]
            rows = pl.ds(field * HALO, HALO)
            pair_ref[layer, rows, :] = jnp.where(odd, low, high)
            other_ref[layer, rows, :] = jnp.where(odd, high, low)
        pair_ref[layer, pl.ds(15, 1), :] = jnp.zeros((1, TY), F32)
        other_ref[layer, pl.ds(15, 1), :] = jnp.zeros((1, TY), F32)


def sweeper(
    tile_ref,
    med_ref,
    open_ref,
    med_pair_ref,
    med_other_ref,
    cell_ref,
    weight_ref,
    ext_ref,
    coef_ref,
    grad_ref,
):
    tile = tile_ref[0, 0]
    n_tiles = tile_ref[0, 1]
    whole_x = n_tiles * TX
    odd = tile % 2

    row = lax.broadcasted_iota(jnp.int32, (EXT, TY), 0)
    lane = lax.broadcasted_iota(jnp.int32, (EXT, TY), 1)
    global_x = tile * TX + row - OFF
    live = (global_x >= 0) & (global_x < whole_x)
    live_next = (global_x + 1 >= 0) & (global_x + 1 < whole_x)
    both = jnp.where(live & live_next, 1.0, 0.0).astype(F32)
    for layer in range(LAY):
        for field in range(5):
            fill = jnp.ones((OFF, TY), F32)
            ext_ref[field, layer, pl.ds(0, OFF), :] = fill
            ext_ref[field, layer, pl.ds(OFF + TX, OFF), :] = fill
            own = med_ref[layer, field] if field < 4 else open_ref[layer].astype(F32)
            ext_ref[field, layer, pl.ds(OFF, TX), :] = own
            if med_pair_ref is None:
                continue
            pair = med_pair_ref[layer, pl.ds(field * HALO, HALO), :]
            other = med_other_ref[layer, pl.ds(field * HALO, HALO), :]
            ext_ref[field, layer, pl.ds(OFF - HALO, HALO), :] = jnp.where(odd == 1, pair, other)
            ext_ref[field, layer, pl.ds(OFF + TX, HALO), :] = jnp.where(odd == 1, other, pair)

    def medium(field, layer):
        value = ext_ref[field, layer]
        if field < 3:
            return jnp.where(live, value, 1.0)
        return value

    def below(value):
        return pltpu.roll(value, 1, 0)

    def above(value):
        return pltpu.roll(value, EXT - 1, 0)

    def west(value):
        return pltpu.roll(value, 1, 1)

    def east(value):
        return pltpu.roll(value, TY - 1, 1)

    has_west = jnp.where(lane > 0, 1.0, 0.0).astype(F32)
    has_east = jnp.where(lane < TY - 1, 1.0, 0.0).astype(F32)
    before = below(both)

    def faces(mine, other):
        inv = 1.0 / (mine + other)
        face = 2.0 * mine * other * inv
        return face, face * other * inv

    for layer in range(LAY):
        k = medium(0, layer)
        kv = medium(1, layer)
        head = medium(3, layer)
        fxm, gxm = faces(k, below(k))
        fxp, gxp = faces(k, above(k))
        fym, gym = faces(k, west(k))
        fyp, gyp = faces(k, east(k))
        fxm = fxm * before
        fxp = fxp * both
        fym = fym * has_west
        fyp = fyp * has_east
        diag = medium(2, layer) + fxm + fxp + fym + fyp
        zero = jnp.zeros((EXT, TY), F32)
        fzm = fzp = gzm = gzp = zero
        if layer > 0:
            fzm, gzm = faces(kv, medium(1, layer - 1))
            gate = ext_ref[4, layer - 1]
            fzm = fzm * gate
            gzm = gzm * gate * (head - medium(3, layer - 1))
        if layer < LAY - 1:
            fzp, gzp = faces(kv, medium(1, layer + 1))
            gate = ext_ref[4, layer]
            fzp = fzp * gate
            gzp = gzp * gate * (head - medium(3, layer + 1))
        diag = diag + fzm + fzp
        scale = OMEGA / diag
        for n, value in enumerate((fxm, fxp, fym, fyp, fzm, fzp)):
            coef_ref[n, layer] = value * scale
        coef_ref[6, layer] = scale
        if grad_ref is None:
            continue
        grad_ref[0, layer] = gxm * before * (head - below(head))
        grad_ref[1, layer] = gxp * both * (head - above(head))
        grad_ref[2, layer] = gym * has_west * (head - west(head))
        grad_ref[3, layer] = gyp * has_east * (head - east(head))
        grad_ref[4, layer] = gzm
        grad_ref[5, layer] = gzp

    lanes = lax.broadcasted_iota(jnp.int32, (OBS, TY), 1)
    eye = lax.broadcasted_iota(jnp.int32, (OBS, OBS), 0) == lax.broadcasted_iota(
        jnp.int32, (OBS, OBS), 1
    )

    def column(row):
        square = jnp.where(eye, jnp.broadcast_to(row, (OBS, OBS)), 0.0)
        return jnp.broadcast_to(jnp.sum(square, axis=1, keepdims=True), (OBS, TY))

    target = [
        column(cell_ref[pl.ds(m, 1), :].astype(F32)).astype(jnp.int32) - lanes for m in range(2)
    ]
    amount = [column(weight_ref[pl.ds(m, 1), :]) for m in range(2)]

    def rows(ref, n, layer, x):
        return jnp.broadcast_to(ref[n, layer, pl.ds(x + OFF, 1), :], (OBS, TY))

    def sweep(src, columns, store):
        def body(layer, carry):
            down = jnp.maximum(layer - 1, 0)
            up = jnp.minimum(layer + 1, LAY - 1)
            for x in columns:
                mid = src(layer, x)
                base = (layer * whole_x + tile * TX + x) * TY
                source = jnp.where(target[0] == base, amount[0], 0.0) + jnp.where(
                    target[1] == base, amount[1], 0.0
                )
                value = (1.0 - OMEGA) * mid + rows(coef_ref, 6, layer, x) * source
                value += rows(coef_ref, 0, layer, x) * src(layer, x - 1)
                value += rows(coef_ref, 1, layer, x) * src(layer, x + 1)
                value += rows(coef_ref, 2, layer, x) * pltpu.roll(mid, 1, 1)
                value += rows(coef_ref, 3, layer, x) * pltpu.roll(mid, TY - 1, 1)
                value += rows(coef_ref, 4, layer, x) * src(down, x)
                value += rows(coef_ref, 5, layer, x) * src(up, x)
                store(layer, x, value)
            return carry

        lax.fori_loop(0, LAY, body, 0)

    return rows, sweep


def interior_kernel(
    tile_ref, turned_ref, med_ref, open_ref, cell_ref, weight_ref, out_ref, ext_ref, coef_ref
):
    _, sweep = sweeper(
        tile_ref, med_ref, open_ref, None, None, cell_ref, weight_ref, ext_ref, coef_ref, None
    )

    def store(layer, x, value):
        out_ref[layer, x - 1] = value

    sweep(lambda layer, x: turned_ref[layer, x], range(1, TX - 1), store)


def stencil_kernel(
    tile_ref,
    turned_ref,
    pair_ref,
    other_ref,
    med_ref,
    open_ref,
    med_pair_ref,
    med_other_ref,
    cell_ref,
    weight_ref,
    inner_ref,
    out_ref,
    ext_ref,
    coef_ref,
    grad_ref,
    halo_ref,
    rim_ref,
    two_ref,
):
    odd = tile_ref[0, 0] % 2
    rows, sweep = sweeper(
        tile_ref,
        med_ref,
        open_ref,
        med_pair_ref,
        med_other_ref,
        cell_ref,
        weight_ref,
        ext_ref,
        coef_ref,
        grad_ref,
    )

    def place(layer, carry):
        for j in range(HALO):
            halo_ref[layer, HALO * (1 - odd) + j] = pair_ref[layer, j]
            halo_ref[layer, HALO * odd + j] = other_ref[layer, j]
        return carry

    lax.fori_loop(0, LAY, place, 0)

    def start(layer, x):
        if x < 0:
            return halo_ref[layer, x + HALO]
        if x < TX:
            return turned_ref[layer, x]
        return halo_ref[layer, x + HALO - TX]

    def rim(x):
        return x + 2 if x < 1 else x - TX + 4

    def one(layer, x):
        if 1 <= x < TX - 1:
            return inner_ref[layer, x - 1]
        return rim_ref[layer, rim(x)]

    def store_rim(layer, x, value):
        rim_ref[layer, rim(x)] = value

    def store_two(layer, x, value):
        two_ref[layer, x + 1] = value

    sweep(start, (-2, -1, 0, TX - 1, TX, TX + 1), store_rim)
    sweep(one, range(-1, TX + 1), store_two)

    def sense(layer, carry):
        down = jnp.maximum(layer - 1, 0)
        up = jnp.minimum(layer + 1, LAY - 1)
        for x in range(TX):
            j = x + 1
            mid = two_ref[layer, j]
            horiz = rows(grad_ref, 0, layer, x) * (two_ref[layer, j - 1] - mid)
            horiz += rows(grad_ref, 1, layer, x) * (two_ref[layer, j + 1] - mid)
            horiz += rows(grad_ref, 2, layer, x) * (pltpu.roll(mid, 1, 1) - mid)
            horiz += rows(grad_ref, 3, layer, x) * (pltpu.roll(mid, TY - 1, 1) - mid)
            vert = rows(grad_ref, 4, layer, x) * (two_ref[down, j] - mid)
            vert += rows(grad_ref, 5, layer, x) * (two_ref[up, j] - mid)
            chunk = layer * (TX // 2) + x // 2
            half = pl.ds((x % 2) * TY, TY)
            out_ref[chunk, pl.ds(0, OBS), half] = horiz
            out_ref[chunk, pl.ds(OBS, OBS), half] = vert
        return carry

    lax.fori_loop(0, LAY, sense, 0)


def krig_kernel(tile_ref, sens_ref, pilot_ref, med_ref, *rest):
    swap_ref, send_ref, late_ref, own_ref, index_ref, share_ref, total_ref = rest
    tile = tile_ref[0, 0]
    base = (tile - RADIUS) * P_DEV
    chunks = LAY * TX // KX

    for layer in range(LAY):
        index = [pilot_ref[k, layer] - base for k in range(NK)]
        share = [med_ref[layer, 4 + k] for k in range(NK)]
        for k in range(1, NK):
            for j in range(k):
                same = index[j] == index[k]
                share[j] = share[j] + jnp.where(same, share[k], 0.0)
                index[k] = jnp.where(same, -1, index[k])
        for k in range(NK):
            index_ref[k, pl.ds(layer * TX, TX), :] = index[k]
            share_ref[k, pl.ds(layer * TX, TX), :] = share[k]

    iota = lax.broadcasted_iota(I16, (16, TY), 0)
    total_ref[...] = jnp.zeros_like(total_ref)

    def split(value):
        high = value.astype(BF16)
        return high, (value - high.astype(F32)).astype(BF16)

    def body(chunk, carry):
        columns = []
        for s in range(KX):
            row = pl.ds(chunk * KX + s, 1)
            index = []
            high = []
            low = []
            for k in range(NK):
                index.append(jnp.broadcast_to(index_ref[k, row, :], (16, TY)).astype(I16))
                first, second = split(jnp.broadcast_to(share_ref[k, row, :], (16, TY)))
                high.append(first)
                low.append(second)
            uppers = []
            lowers = []
            for i in range(SPAN // 16):
                pilot = iota + I16(16 * i)
                upper = jnp.zeros((16, TY), BF16)
                lower = jnp.zeros((16, TY), BF16)
                for k in range(NK):
                    hit = index[k] == pilot
                    upper = jnp.where(hit, high[k], upper)
                    lower = jnp.where(hit, low[k], lower)
                uppers.append(upper)
                lowers.append(lower)
            columns.append(jnp.concatenate(uppers + lowers, axis=0))
        sens = []
        for q in range(KX // 2):
            sens.append(jnp.concatenate(split(sens_ref[chunk * (KX // 2) + q]), axis=0))
        total_ref[...] += lax.dot_general(
            jnp.concatenate(columns, axis=1),
            jnp.concatenate(sens, axis=1),
            (((1,), (1,)), ((), ())),
            preferred_element_type=F32,
        )
        return carry

    lax.fori_loop(0, chunks, body, 0)

    def piece(o):
        start = pl.multiple_of(o * P_DEV, P_DEV)
        value = total_ref[pl.ds(start, P_DEV), :] + total_ref[pl.ds(SPAN + start, P_DEV), :]
        value = value.T
        return value[: 2 * OBS] + value[2 * OBS :]

    odd = tile % 2
    swap_ref[...] = piece((1 - odd) * 4)
    send_ref[pl.ds(0, 2 * OBS), :] = piece(1 + 2 * odd)
    send_ref[pl.ds(2 * OBS, 2 * OBS), :] = piece(4 * odd)
    late_ref[...] = piece(3 - 2 * odd)
    own_ref[...] = piece(RADIUS)


def in_hbm(array):
    return pltpu.with_memory_space_constraint(array, pltpu.HBM)


def swapped(block):
    count = lax.axis_size("grid")
    return lax.ppermute(block, "grid", [(i, i ^ 1) for i in range(count)])


def crossed(block):
    count = lax.axis_size("grid")
    pairs = [(i, i + 1 if i % 2 else i - 1) for i in range(1, count - 1)]
    return lax.ppermute(block, "grid", pairs)


def gathered(copies, axis):
    return lax.all_to_all(copies, axis, 0, 0, tiled=False)


def local(
    adjoint_start,
    conductance,
    storage,
    head,
    layer_open,
    krig_weight,
    krig_pilot,
    obs_cell,
    obs_weight,
):
    sds = jax.ShapeDtypeStruct
    tile = jnp.stack([lax.axis_index("grid"), jnp.int32(lax.axis_size("grid"))]).reshape(1, 2)

    copies = pltpu.HBM((LAY, 4 + NK, TX, TY), F32)
    copies = pl.pallas_call(
        spread_kernel,
        out_shape=copies,
        in_specs=[HBM] * 4,
        out_specs=HBM,
        scratch_shapes=[pltpu.SemaphoreType.DMA((4 * LAY,))],
        compiler_params=pltpu.CompilerParams(vmem_limit_bytes=4 * 2**20),
    )(*map(in_hbm, (conductance, storage, head, krig_weight)))
    medium = gathered(copies, "obs")

    edge = sds((LAY, HALO, OBS, TY), F32)
    turned, pair, other = pl.pallas_call(
        turn_kernel,
        out_shape=(sds((LAY, TX, OBS, TY), F32), edge, edge),
        in_specs=[SMEM, HBM],
        out_specs=(VMEM, VMEM, VMEM),
        scratch_shapes=[
            pltpu.VMEM((LAY, OBS, TX, TY), F32),
            pltpu.SemaphoreType.DMA((LAY,)),
        ],
        compiler_params=pltpu.CompilerParams(vmem_limit_bytes=12 * 2**20),
    )(tile, in_hbm(adjoint_start))
    other = crossed(other)
    pair = swapped(pair)

    edge = sds((LAY, 16, TY), F32)
    med_pair, med_other = pl.pallas_call(
        medium_edges_kernel,
        out_shape=(edge, edge),
        in_specs=[SMEM, VMEM, VMEM],
        out_specs=(VMEM, VMEM),
        compiler_params=pltpu.CompilerParams(vmem_limit_bytes=8 * 2**20),
    )(tile, medium, layer_open)
    med_other = crossed(med_other)
    med_pair = swapped(med_pair)

    cells = obs_cell.T
    amounts = obs_weight.T
    inner = pl.pallas_call(
        interior_kernel,
        out_shape=sds((LAY, TX - 2, OBS, TY), F32),
        in_specs=[SMEM] + [VMEM] * 5,
        out_specs=VMEM,
        scratch_shapes=[
            pltpu.VMEM((5, LAY, EXT, TY), F32),
            pltpu.VMEM((7, LAY, EXT, TY), F32),
        ],
        compiler_params=pltpu.CompilerParams(vmem_limit_bytes=16 * 2**20),
    )(tile, turned, medium, layer_open, cells, amounts)

    sens = pl.pallas_call(
        stencil_kernel,
        out_shape=sds((LAY * TX // 2, 2 * OBS, 2 * TY), F32),
        in_specs=[SMEM] + [VMEM] * 10,
        out_specs=VMEM,
        scratch_shapes=[
            pltpu.VMEM((5, LAY, EXT, TY), F32),
            pltpu.VMEM((7, LAY, EXT, TY), F32),
            pltpu.VMEM((6, LAY, EXT, TY), F32),
            pltpu.VMEM((LAY, 2 * HALO, OBS, TY), F32),
            pltpu.VMEM((LAY, 2 * HALO, OBS, TY), F32),
            pltpu.VMEM((LAY, TX + 2, OBS, TY), F32),
        ],
        compiler_params=pltpu.CompilerParams(vmem_limit_bytes=24 * 2**20),
    )(
        tile,
        turned,
        pair,
        other,
        medium,
        layer_open,
        med_pair,
        med_other,
        cells,
        amounts,
        inner,
    )

    piece = sds((2 * OBS, P_DEV), F32)
    swap, send, late, owned = pl.pallas_call(
        krig_kernel,
        out_shape=(piece, sds((4 * OBS, P_DEV), F32), piece, piece),
        in_specs=[SMEM] + [VMEM] * 3,
        out_specs=(VMEM,) * 4,
        scratch_shapes=[
            pltpu.VMEM((NK, LAY * TX, TY), jnp.int32),
            pltpu.VMEM((NK, LAY * TX, TY), F32),
            pltpu.VMEM((2 * SPAN, 4 * OBS), F32),
        ],
        compiler_params=pltpu.CompilerParams(vmem_limit_bytes=24 * 2**20),
    )(tile, sens, krig_pilot, medium)

    half = 2 * OBS
    arrived = crossed(jnp.concatenate([send[:half] + swapped(swap), send[half:]], axis=0))
    owned = owned + arrived[:half] + swapped(late + arrived[half:])
    return owned.reshape(2, OBS, P_DEV)


def solution(mesh):
    return jax.shard_map(
        local,
        mesh=mesh,
        in_specs=(
            P("obs", None, "grid", None),
            P(None, "obs", "grid", None),
            P("obs", "grid", None),
            P("obs", "grid", None),
            P(None, "grid", None),
            P(None, "obs", "grid", None),
            P(None, None, "grid", None),
            P("obs", None),
            P("obs", None),
        ),
        out_specs=P(None, "obs", "grid"),
        check_vma=False,
    )
```

```python
import jax
import jax.numpy as jnp
from jax import lax
from jax.experimental import pallas as pl
from jax.experimental.pallas import tpu as pltpu
from jax.sharding import PartitionSpec as P


NK = 4
RADIUS = 2
P_DEV = 128
OMEGA = 0.8
LAY = 8
OBS = 32
TX = 16
TY = 128
HALO = 3
SPAN = (2 * RADIUS + 1) * P_DEV
OFF = 8
EXT = 32
KX = 16

F32 = jnp.float32
BF16 = jnp.bfloat16
I16 = jnp.int16
VMEM = pl.BlockSpec(memory_space=pltpu.VMEM)
SMEM = pl.BlockSpec(memory_space=pltpu.SMEM)
HBM = pl.BlockSpec(memory_space=pltpu.HBM)


def spread_kernel(cond_ref, storage_ref, head_ref, krig_ref, med_ref, own_ref, in_ref, out_ref):
    parts = (
        (cond_ref.at[:, 0], own_ref.at[pl.ds(0, 2)]),
        (storage_ref, own_ref.at[pl.ds(2, 1)]),
        (head_ref, own_ref.at[pl.ds(3, 1)]),
        (krig_ref.at[:, 0], own_ref.at[pl.ds(4, NK)]),
    )
    loads = [
        pltpu.make_async_copy(part, place, in_ref.at[i]) for i, (part, place) in enumerate(parts)
    ]
    for load in loads:
        load.start()
    for load in loads:
        load.wait()
    stores = [
        pltpu.make_async_copy(own_ref, med_ref.at[layer], out_ref.at[layer])
        for layer in range(LAY)
    ]
    for store in stores:
        store.start()
    for store in stores:
        store.wait()


def turn_kernel(tile_ref, adj_ref, turned_ref, pair_ref, other_ref, buf_ref, sem_ref):
    odd = tile_ref[0, 0] % 2
    pair_start = (1 - odd) * (TX - HALO)
    other_start = odd * (TX - HALO)

    def fetch(layer):
        return pltpu.make_async_copy(
            adj_ref.at[:, layer], buf_ref.at[layer], sem_ref.at[layer]
        )

    for layer in range(LAY):
        fetch(layer).start()

    def body(layer, carry):
        fetch(layer).wait()
        rows_ref = buf_ref.at[layer].reshape(OBS * TX, TY)
        for x in range(TX):
            turned_ref[layer, x] = rows_ref[pl.ds(x, OBS, stride=TX), :]
        for j in range(HALO):
            pair_ref[layer, j] = turned_ref[layer, pair_start + j]
            other_ref[layer, j] = turned_ref[layer, other_start + j]
        return carry

    lax.fori_loop(0, LAY, body, 0)


def place_of(layer, odd):
    return layer + odd * (LAY - 1 - 2 * layer)


def medium_edges_kernel(tile_ref, med_ref, open_ref, pair_ref, other_ref):
    parity = tile_ref[0, 0] % 2
    odd = parity == 1
    for layer in range(LAY):
        place = place_of(layer, parity)
        for field in range(5):
            if field < 4:
                tile = med_ref[place, field]
            else:
                tile = open_ref[layer].astype(F32)
            low = tile[:HALO]
            high = tile[TX - HALO :]
            rows = pl.ds(field * HALO, HALO)
            pair_ref[layer, rows, :] = jnp.where(odd, low, high)
            other_ref[layer, rows, :] = jnp.where(odd, high, low)
        pair_ref[layer, pl.ds(15, 1), :] = jnp.zeros((1, TY), F32)
        other_ref[layer, pl.ds(15, 1), :] = jnp.zeros((1, TY), F32)


def sweeper(
    tile_ref,
    med_ref,
    open_ref,
    med_pair_ref,
    med_other_ref,
    cell_ref,
    weight_ref,
    ext_ref,
    coef_ref,
    grad_ref,
):
    tile = tile_ref[0, 0]
    n_tiles = tile_ref[0, 1]
    whole_x = n_tiles * TX
    odd = tile % 2

    row = lax.broadcasted_iota(jnp.int32, (EXT, TY), 0)
    lane = lax.broadcasted_iota(jnp.int32, (EXT, TY), 1)
    global_x = tile * TX + row - OFF
    live = (global_x >= 0) & (global_x < whole_x)
    live_next = (global_x + 1 >= 0) & (global_x + 1 < whole_x)
    both = jnp.where(live & live_next, 1.0, 0.0).astype(F32)
    for layer in range(LAY):
        for field in range(5):
            fill = jnp.ones((OFF, TY), F32)
            ext_ref[field, layer, pl.ds(0, OFF), :] = fill
            ext_ref[field, layer, pl.ds(OFF + TX, OFF), :] = fill
            own = med_ref[place_of(layer, odd), field] if field < 4 else open_ref[layer].astype(F32)
            ext_ref[field, layer, pl.ds(OFF, TX), :] = own
            if med_pair_ref is None:
                continue
            pair = med_pair_ref[layer, pl.ds(field * HALO, HALO), :]
            other = med_other_ref[layer, pl.ds(field * HALO, HALO), :]
            ext_ref[field, layer, pl.ds(OFF - HALO, HALO), :] = jnp.where(odd == 1, pair, other)
            ext_ref[field, layer, pl.ds(OFF + TX, HALO), :] = jnp.where(odd == 1, other, pair)

    def medium(field, layer):
        value = ext_ref[field, layer]
        if field < 3:
            return jnp.where(live, value, 1.0)
        return value

    def below(value):
        return pltpu.roll(value, 1, 0)

    def above(value):
        return pltpu.roll(value, EXT - 1, 0)

    def west(value):
        return pltpu.roll(value, 1, 1)

    def east(value):
        return pltpu.roll(value, TY - 1, 1)

    has_west = jnp.where(lane > 0, 1.0, 0.0).astype(F32)
    has_east = jnp.where(lane < TY - 1, 1.0, 0.0).astype(F32)
    before = below(both)

    def faces(mine, other):
        inv = 1.0 / (mine + other)
        face = 2.0 * mine * other * inv
        return face, face * other * inv

    for layer in range(LAY):
        k = medium(0, layer)
        kv = medium(1, layer)
        head = medium(3, layer)
        fxm, gxm = faces(k, below(k))
        fxp, gxp = faces(k, above(k))
        fym, gym = faces(k, west(k))
        fyp, gyp = faces(k, east(k))
        fxm = fxm * before
        fxp = fxp * both
        fym = fym * has_west
        fyp = fyp * has_east
        diag = medium(2, layer) + fxm + fxp + fym + fyp
        zero = jnp.zeros((EXT, TY), F32)
        fzm = fzp = gzm = gzp = zero
        if layer > 0:
            fzm, gzm = faces(kv, medium(1, layer - 1))
            gate = ext_ref[4, layer - 1]
            fzm = fzm * gate
            gzm = gzm * gate * (head - medium(3, layer - 1))
        if layer < LAY - 1:
            fzp, gzp = faces(kv, medium(1, layer + 1))
            gate = ext_ref[4, layer]
            fzp = fzp * gate
            gzp = gzp * gate * (head - medium(3, layer + 1))
        diag = diag + fzm + fzp
        scale = OMEGA / diag
        for n, value in enumerate((fxm, fxp, fym, fyp, fzm, fzp)):
            coef_ref[n, layer] = value * scale
        coef_ref[6, layer] = scale
        if grad_ref is None:
            continue
        grad_ref[0, layer] = gxm * before * (head - below(head))
        grad_ref[1, layer] = gxp * both * (head - above(head))
        grad_ref[2, layer] = gym * has_west * (head - west(head))
        grad_ref[3, layer] = gyp * has_east * (head - east(head))
        grad_ref[4, layer] = gzm
        grad_ref[5, layer] = gzp

    lanes = lax.broadcasted_iota(jnp.int32, (OBS, TY), 1)
    eye = lax.broadcasted_iota(jnp.int32, (OBS, OBS), 0) == lax.broadcasted_iota(
        jnp.int32, (OBS, OBS), 1
    )

    def column(row):
        square = jnp.where(eye, jnp.broadcast_to(row, (OBS, OBS)), 0.0)
        return jnp.broadcast_to(jnp.sum(square, axis=1, keepdims=True), (OBS, TY))

    target = [
        column(cell_ref[pl.ds(m, 1), :].astype(F32)).astype(jnp.int32) - lanes for m in range(2)
    ]
    amount = [column(weight_ref[pl.ds(m, 1), :]) for m in range(2)]

    def rows(ref, n, layer, x):
        return jnp.broadcast_to(ref[n, layer, pl.ds(x + OFF, 1), :], (OBS, TY))

    def sweep(src, columns, store):
        def body(layer, carry):
            down = jnp.maximum(layer - 1, 0)
            up = jnp.minimum(layer + 1, LAY - 1)
            for x in columns:
                mid = src(layer, x)
                base = (layer * whole_x + tile * TX + x) * TY
                source = jnp.where(target[0] == base, amount[0], 0.0) + jnp.where(
                    target[1] == base, amount[1], 0.0
                )
                value = (1.0 - OMEGA) * mid + rows(coef_ref, 6, layer, x) * source
                value += rows(coef_ref, 0, layer, x) * src(layer, x - 1)
                value += rows(coef_ref, 1, layer, x) * src(layer, x + 1)
                value += rows(coef_ref, 2, layer, x) * pltpu.roll(mid, 1, 1)
                value += rows(coef_ref, 3, layer, x) * pltpu.roll(mid, TY - 1, 1)
                value += rows(coef_ref, 4, layer, x) * src(down, x)
                value += rows(coef_ref, 5, layer, x) * src(up, x)
                store(layer, x, value)
            return carry

        lax.fori_loop(0, LAY, body, 0)

    return rows, sweep


def interior_kernel(
    tile_ref, turned_ref, med_ref, open_ref, cell_ref, weight_ref, out_ref, ext_ref, coef_ref
):
    _, sweep = sweeper(
        tile_ref, med_ref, open_ref, None, None, cell_ref, weight_ref, ext_ref, coef_ref, None
    )

    def store(layer, x, value):
        out_ref[layer, x - 1] = value

    sweep(lambda layer, x: turned_ref[layer, x], range(1, TX - 1), store)


def stencil_kernel(
    tile_ref,
    turned_ref,
    pair_ref,
    other_ref,
    med_ref,
    open_ref,
    med_pair_ref,
    med_other_ref,
    cell_ref,
    weight_ref,
    inner_ref,
    out_ref,
    ext_ref,
    coef_ref,
    grad_ref,
    halo_ref,
    rim_ref,
    two_ref,
):
    odd = tile_ref[0, 0] % 2
    rows, sweep = sweeper(
        tile_ref,
        med_ref,
        open_ref,
        med_pair_ref,
        med_other_ref,
        cell_ref,
        weight_ref,
        ext_ref,
        coef_ref,
        grad_ref,
    )

    def place(layer, carry):
        for j in range(HALO):
            halo_ref[layer, HALO * (1 - odd) + j] = pair_ref[layer, j]
            halo_ref[layer, HALO * odd + j] = other_ref[layer, j]
        return carry

    lax.fori_loop(0, LAY, place, 0)

    def start(layer, x):
        if x < 0:
            return halo_ref[layer, x + HALO]
        if x < TX:
            return turned_ref[layer, x]
        return halo_ref[layer, x + HALO - TX]

    def rim(x):
        return x + 2 if x < 1 else x - TX + 4

    def one(layer, x):
        if 1 <= x < TX - 1:
            return inner_ref[layer, x - 1]
        return rim_ref[layer, rim(x)]

    def store_rim(layer, x, value):
        rim_ref[layer, rim(x)] = value

    def store_two(layer, x, value):
        two_ref[layer, x + 1] = value

    sweep(start, (-2, -1, 0, TX - 1, TX, TX + 1), store_rim)
    sweep(one, range(-1, TX + 1), store_two)

    def sense(layer, carry):
        down = jnp.maximum(layer - 1, 0)
        up = jnp.minimum(layer + 1, LAY - 1)
        for x in range(TX):
            j = x + 1
            mid = two_ref[layer, j]
            horiz = rows(grad_ref, 0, layer, x) * (two_ref[layer, j - 1] - mid)
            horiz += rows(grad_ref, 1, layer, x) * (two_ref[layer, j + 1] - mid)
            horiz += rows(grad_ref, 2, layer, x) * (pltpu.roll(mid, 1, 1) - mid)
            horiz += rows(grad_ref, 3, layer, x) * (pltpu.roll(mid, TY - 1, 1) - mid)
            vert = rows(grad_ref, 4, layer, x) * (two_ref[down, j] - mid)
            vert += rows(grad_ref, 5, layer, x) * (two_ref[up, j] - mid)
            chunk = layer * (TX // 2) + x // 2
            half = pl.ds((x % 2) * TY, TY)
            out_ref[chunk, pl.ds(0, OBS), half] = horiz
            out_ref[chunk, pl.ds(OBS, OBS), half] = vert
        return carry

    lax.fori_loop(0, LAY, sense, 0)


def krig_kernel(tile_ref, sens_ref, pilot_ref, med_ref, *rest):
    swap_ref, send_ref, late_ref, own_ref, index_ref, share_ref, total_ref = rest
    tile = tile_ref[0, 0]
    base = (tile - RADIUS) * P_DEV
    chunks = LAY * TX // KX

    for layer in range(LAY):
        index = [pilot_ref[k, layer] - base for k in range(NK)]
        place = place_of(layer, tile % 2)
        share = [med_ref[place, 4 + k] for k in range(NK)]
        for k in range(1, NK):
            for j in range(k):
                same = index[j] == index[k]
                share[j] = share[j] + jnp.where(same, share[k], 0.0)
                index[k] = jnp.where(same, -1, index[k])
        for k in range(NK):
            index_ref[k, pl.ds(layer * TX, TX), :] = index[k]
            share_ref[k, pl.ds(layer * TX, TX), :] = share[k]

    iota = lax.broadcasted_iota(I16, (16, TY), 0)
    total_ref[...] = jnp.zeros_like(total_ref)

    def split(value):
        high = value.astype(BF16)
        return high, (value - high.astype(F32)).astype(BF16)

    def body(chunk, carry):
        columns = []
        for s in range(KX):
            row = pl.ds(chunk * KX + s, 1)
            index = []
            high = []
            low = []
            for k in range(NK):
                index.append(jnp.broadcast_to(index_ref[k, row, :], (16, TY)).astype(I16))
                first, second = split(jnp.broadcast_to(share_ref[k, row, :], (16, TY)))
                high.append(first)
                low.append(second)
            uppers = []
            lowers = []
            for i in range(SPAN // 16):
                pilot = iota + I16(16 * i)
                upper = jnp.zeros((16, TY), BF16)
                lower = jnp.zeros((16, TY), BF16)
                for k in range(NK):
                    hit = index[k] == pilot
                    upper = jnp.where(hit, high[k], upper)
                    lower = jnp.where(hit, low[k], lower)
                uppers.append(upper)
                lowers.append(lower)
            columns.append(jnp.concatenate(uppers + lowers, axis=0))
        sens = []
        for q in range(KX // 2):
            sens.append(jnp.concatenate(split(sens_ref[chunk * (KX // 2) + q]), axis=0))
        total_ref[...] += lax.dot_general(
            jnp.concatenate(columns, axis=1),
            jnp.concatenate(sens, axis=1),
            (((1,), (1,)), ((), ())),
            preferred_element_type=F32,
        )
        return carry

    lax.fori_loop(0, chunks, body, 0)

    def piece(o):
        start = pl.multiple_of(o * P_DEV, P_DEV)
        value = total_ref[pl.ds(start, P_DEV), :] + total_ref[pl.ds(SPAN + start, P_DEV), :]
        value = value.T
        return value[: 2 * OBS] + value[2 * OBS :]

    odd = tile % 2
    swap_ref[...] = piece((1 - odd) * 4)
    send_ref[pl.ds(0, 2 * OBS), :] = piece(1 + 2 * odd)
    send_ref[pl.ds(2 * OBS, 2 * OBS), :] = piece(4 * odd)
    late_ref[...] = piece(3 - 2 * odd)
    own_ref[...] = piece(RADIUS)


def in_hbm(array):
    return pltpu.with_memory_space_constraint(array, pltpu.HBM)


def swapped(block):
    count = lax.axis_size("grid")
    return lax.ppermute(block, "grid", [(i, i ^ 1) for i in range(count)])


def crossed(block):
    count = lax.axis_size("grid")
    pairs = [(i, i + 1 if i % 2 else i - 1) for i in range(1, count - 1)]
    return lax.ppermute(block, "grid", pairs)


def gathered(copies):
    layers = lax.axis_size("obs")
    tiles = lax.axis_size("grid")
    groups = [
        [place_of(layer, tile % 2) * tiles + tile for layer in range(layers)]
        for tile in range(tiles)
    ]
    return lax.all_to_all(copies, ("obs", "grid"), 0, 0, axis_index_groups=groups, tiled=False)


def local(
    adjoint_start,
    conductance,
    storage,
    head,
    layer_open,
    krig_weight,
    krig_pilot,
    obs_cell,
    obs_weight,
):
    sds = jax.ShapeDtypeStruct
    tile = jnp.stack([lax.axis_index("grid"), jnp.int32(lax.axis_size("grid"))]).reshape(1, 2)

    copies = pltpu.HBM((LAY, 4 + NK, TX, TY), F32)
    copies = pl.pallas_call(
        spread_kernel,
        out_shape=copies,
        in_specs=[HBM] * 4,
        out_specs=HBM,
        scratch_shapes=[
            pltpu.VMEM((4 + NK, TX, TY), F32),
            pltpu.SemaphoreType.DMA((4,)),
            pltpu.SemaphoreType.DMA((LAY,)),
        ],
        compiler_params=pltpu.CompilerParams(vmem_limit_bytes=4 * 2**20),
    )(*map(in_hbm, (conductance, storage, head, krig_weight)))
    medium = gathered(copies)

    edge = sds((LAY, HALO, OBS, TY), F32)
    turned, pair, other = pl.pallas_call(
        turn_kernel,
        out_shape=(sds((LAY, TX, OBS, TY), F32), edge, edge),
        in_specs=[SMEM, HBM],
        out_specs=(VMEM, VMEM, VMEM),
        scratch_shapes=[
            pltpu.VMEM((LAY, OBS, TX, TY), F32),
            pltpu.SemaphoreType.DMA((LAY,)),
        ],
        compiler_params=pltpu.CompilerParams(vmem_limit_bytes=12 * 2**20),
    )(tile, in_hbm(adjoint_start))
    other = crossed(other)
    pair = swapped(pair)

    edge = sds((LAY, 16, TY), F32)
    med_pair, med_other = pl.pallas_call(
        medium_edges_kernel,
        out_shape=(edge, edge),
        in_specs=[SMEM, VMEM, VMEM],
        out_specs=(VMEM, VMEM),
        compiler_params=pltpu.CompilerParams(vmem_limit_bytes=8 * 2**20),
    )(tile, medium, layer_open)
    med_other = crossed(med_other)
    med_pair = swapped(med_pair)

    cells = obs_cell.T
    amounts = obs_weight.T
    inner = pl.pallas_call(
        interior_kernel,
        out_shape=sds((LAY, TX - 2, OBS, TY), F32),
        in_specs=[SMEM] + [VMEM] * 5,
        out_specs=VMEM,
        scratch_shapes=[
            pltpu.VMEM((5, LAY, EXT, TY), F32),
            pltpu.VMEM((7, LAY, EXT, TY), F32),
        ],
        compiler_params=pltpu.CompilerParams(vmem_limit_bytes=16 * 2**20),
    )(tile, turned, medium, layer_open, cells, amounts)

    sens = pl.pallas_call(
        stencil_kernel,
        out_shape=sds((LAY * TX // 2, 2 * OBS, 2 * TY), F32),
        in_specs=[SMEM] + [VMEM] * 10,
        out_specs=VMEM,
        scratch_shapes=[
            pltpu.VMEM((5, LAY, EXT, TY), F32),
            pltpu.VMEM((7, LAY, EXT, TY), F32),
            pltpu.VMEM((6, LAY, EXT, TY), F32),
            pltpu.VMEM((LAY, 2 * HALO, OBS, TY), F32),
            pltpu.VMEM((LAY, 2 * HALO, OBS, TY), F32),
            pltpu.VMEM((LAY, TX + 2, OBS, TY), F32),
        ],
        compiler_params=pltpu.CompilerParams(vmem_limit_bytes=24 * 2**20),
    )(
        tile,
        turned,
        pair,
        other,
        medium,
        layer_open,
        med_pair,
        med_other,
        cells,
        amounts,
        inner,
    )

    piece = sds((2 * OBS, P_DEV), F32)
    swap, send, late, owned = pl.pallas_call(
        krig_kernel,
        out_shape=(piece, sds((4 * OBS, P_DEV), F32), piece, piece),
        in_specs=[SMEM] + [VMEM] * 3,
        out_specs=(VMEM,) * 4,
        scratch_shapes=[
            pltpu.VMEM((NK, LAY * TX, TY), jnp.int32),
            pltpu.VMEM((NK, LAY * TX, TY), F32),
            pltpu.VMEM((2 * SPAN, 4 * OBS), F32),
        ],
        compiler_params=pltpu.CompilerParams(vmem_limit_bytes=24 * 2**20),
    )(tile, sens, krig_pilot, medium)

    half = 2 * OBS
    arrived = crossed(jnp.concatenate([send[:half] + swapped(swap), send[half:]], axis=0))
    owned = owned + arrived[:half] + swapped(late + arrived[half:])
    return owned.reshape(2, OBS, P_DEV)


def solution(mesh):
    return jax.shard_map(
        local,
        mesh=mesh,
        in_specs=(
            P("obs", None, "grid", None),
            P(None, "obs", "grid", None),
            P("obs", "grid", None),
            P("obs", "grid", None),
            P(None, "grid", None),
            P(None, "obs", "grid", None),
            P(None, None, "grid", None),
            P("obs", None),
            P("obs", None),
        ),
        out_specs=P(None, "obs", "grid"),
        check_vma=False,
    )
```
